32 devices in a mesh: tm: 2 (over x), slab: 16 (over z, y, core).
Axes of the slice: x: 2, y: 2, z: 4, core: 2. Of those that a mesh axis runs over, the one named last changes fastest.
Arguments:
- volumes: bfloat16 [16, 1024, 64, 128], P('tm', 'slab'), parts along dimension 0, may hold values from -6 to 6
- pair_fields: int32 [8, 128], P(None, ('tm', 'slab')), parts along dimension 1, may hold values from -16 to 64, as said below
- pair_counts: int32 [32], P(('tm', 'slab')), parts along dimension 0, may hold values from 1 to 4, as said below
Outputs:
- correlation: float32 [128, 512], P(('tm', 'slab')), parts along dimension 0
- shifts: float32 [3, 128], P(None, ('tm', 'slab')), parts along dimension 1
- normal_sums: float32 [16, 4, 4], P('tm'), parts along dimension 0
- rhs_sums: float32 [16, 4, 3], P('tm'), parts along dimension 0
The draws below stay inside these ranges and needn't reach their ends.
There are 2 independent parts, one for each index of `tm`. The reference program is written for one: setup_inputs(seed, part) draws one part's arguments, and reference() takes and returns one part's arrays. A program takes and returns all parts, laid end to end along the dimension named above; each array names one. Nothing has to cross between parts.
Inputs may be any that keep to these rules, and one draw needn't show every extreme that they name: `pair_fields`: column p belongs to slab p // 4. Rows: first view; x anchor of its block (0 to 64); second view, the first plus or minus one modulo 8; slab offset of the second block (-1, 0 or 1, never leading outside the volume; 0 in dead columns); x anchor of the second block (0 to 64); window offsets along z, y, x (-16 to 8). Among one slab's live pairs at most 2 have slab offset 1 and at most 2 have -1; in every draw some slab has exactly 2 of each. The first pair of the first slab has slab offset 1 and the first pair of the last slab has -1. `pair_counts`: the live pairs of a slab fill its first slots; in every draw some slab has 4.
All inputs are finite; a program needn't handle non-finite values.
Results may differ from the reference program's by a relative error of at most 0.0003.
Values may be sent and summed in bfloat16 or wider, within the bound.
A program may use at most 128 MiB of HBM per device.

```python
import jax
import jax.numpy as jnp
from jax import lax

VIEWS = 8
B = 64
WIN = 8
CAP = 4
NBR = 2
N_SLAB = 16


def pair_plan(key):
    base = jax.random.fold_in(key, 917)
    keys = jax.random.split(base, 9)
    slab_ids = jnp.arange(N_SLAB, dtype=jnp.int32)
    full_slab = jax.random.randint(keys[0], (), 1, N_SLAB - 1)
    heavy = jax.random.randint(keys[1], (N_SLAB,), 0, 8) == 0
    light = jax.random.randint(keys[2], (N_SLAB,), 1, CAP // 2 + 1)
    counts = jnp.where(heavy | (slab_ids == full_slab), CAP, light).astype(jnp.int32)
    pair_total = N_SLAB * CAP
    owner = jnp.arange(pair_total, dtype=jnp.int32) // CAP
    slot_index = jnp.arange(pair_total, dtype=jnp.int32) % CAP
    first_view = jax.random.randint(keys[3], (pair_total,), 0, VIEWS)
    step_sign = 2 * jax.random.randint(keys[4], (pair_total,), 0, 2) - 1
    second_view = jnp.mod(first_view + step_sign, VIEWS)
    first_x = jax.random.randint(keys[5], (pair_total,), 0, B + 1)
    second_x = jax.random.randint(keys[6], (pair_total,), 0, B + 1)
    offsets = jax.random.randint(keys[7], (3, pair_total), -2 * WIN, WIN + 1)
    direction = jax.random.randint(keys[8], (pair_total,), -1, 2)
    live = slot_index < counts[owner]
    direction = jnp.where(live, direction, 0)
    direction = jnp.where((owner == 0) & (direction < 0), 0, direction)
    direction = jnp.where((owner == N_SLAB - 1) & (direction > 0), 0, direction)
    direction = jnp.where((owner == 0) & (slot_index == 0), 1, direction)
    direction = jnp.where((owner == N_SLAB - 1) & (slot_index == 0), -1, direction)
    grid = direction.reshape(N_SLAB, CAP)
    up_rank = jnp.cumsum((grid == 1).astype(jnp.int32), axis=1)
    down_rank = jnp.cumsum((grid == -1).astype(jnp.int32), axis=1)
    grid = jnp.where((grid == 1) & (up_rank > NBR), 0, grid)
    grid = jnp.where((grid == -1) & (down_rank > NBR), 0, grid)
    slot_ids = jnp.arange(CAP, dtype=jnp.int32)
    forced = jnp.where(slot_ids < NBR, 1, jnp.where(slot_ids < 2 * NBR, -1, 0))
    grid = jnp.where((slab_ids == full_slab)[:, None], forced[None, :], grid)
    direction = grid.reshape(-1)
    fields = jnp.stack([first_view, first_x, second_view, direction, second_x, offsets[0], offsets[1], offsets[2]]).astype(jnp.int32)
    return (fields, counts)


def draw_pair_fields(key, part):
    return pair_plan(key)[0]


def draw_pair_counts(key, part):
    return pair_plan(key)[1]


def block_levels(rng, dims, shards, least, top_value):
    level, own = 1.0, jax.random.fold_in(rng, 6)
    for position, blocks in shards:
        draws = jnp.exp(jax.random.uniform(jax.random.fold_in(own, position), (blocks,), jnp.float32, least / len(shards), top_value / len(shards)))
        level = level * jnp.repeat(draws, dims[position] // blocks).reshape([-1 if axis == position else 1 for axis in range(len(dims))])
    return level


def centred(key, extent, scale, limit, cuts=(), held_as=jnp.bfloat16):
    loudness = block_levels(key, extent, cuts, -0.22, 0.18) if cuts else 1.0
    entries = jax.random.normal(key, extent, jnp.float32) * scale * loudness
    return jnp.minimum(jnp.maximum(entries, -limit), limit).astype(held_as)


def setup_inputs(seed: int = 0, part: int = 0) -> dict:
    arg_keys = jax.random.split(jax.random.key(seed), 4)
    own_keys = jax.random.split(jax.random.fold_in(arg_keys[3], part), 4)
    return {
        "volumes": centred(own_keys[0], (VIEWS, B * N_SLAB, B, 2 * B), 1.0, 6.0, ((1, 16),)),
        "pair_fields": draw_pair_fields(jax.random.fold_in(jax.random.fold_in(arg_keys[3], part), 71), part),
        "pair_counts": draw_pair_counts(jax.random.fold_in(jax.random.fold_in(arg_keys[3], part), 71), part),
    }


EPSILON = 1e-6


def reference(volumes, pair_fields, pair_counts):
    pair_total = CAP * N_SLAB
    window_steps = jnp.arange(WIN, dtype=jnp.int32)
    view_ids = jnp.arange(VIEWS, dtype=jnp.int32)

    def one_pair(pair_index):
        slab_pos = (pair_index // CAP).astype(jnp.int32)
        slot_index = pair_index % CAP
        column = pair_fields[:, pair_index]
        live_mask = (slot_index < pair_counts[slab_pos]).astype(jnp.float32)
        start_a = (slab_pos * B).astype(jnp.int32)
        start_b = ((slab_pos + column[3]) * B).astype(jnp.int32)
        block_a = lax.dynamic_slice(volumes, (column[0].astype(jnp.int32), start_a, jnp.zeros((), jnp.int32), column[1].astype(jnp.int32)), (1, B, B, B))[0].astype(jnp.float32)
        block_b = lax.dynamic_slice(volumes, (column[2].astype(jnp.int32), start_b, jnp.zeros((), jnp.int32), column[4].astype(jnp.int32)), (1, B, B, B))[0].astype(jnp.float32)
        spec_a = jnp.fft.fftn(block_a)
        spec_b = jnp.fft.fftn(block_b)
        cross_term = spec_a * jnp.conj(spec_b)
        magnitude = jnp.abs(cross_term)
        ratio_term = cross_term / (magnitude + (jnp.mean(magnitude) + EPSILON))
        full_corr = jnp.real(jnp.fft.ifftn(ratio_term)) * B ** 1.5
        idx_z = jnp.mod(column[5] + window_steps, B)
        idx_y = jnp.mod(column[6] + window_steps, B)
        idx_x = jnp.mod(column[7] + window_steps, B)
        values = full_corr[idx_z][:, idx_y][:, :, idx_x] * live_mask
        weight = values * values
        energy = jnp.mean(weight)
        steps_f = jnp.arange(WIN, dtype=jnp.float32)
        along_z = (column[5].astype(jnp.float32) + steps_f)[:, None, None]
        along_y = (column[6].astype(jnp.float32) + steps_f)[None, :, None]
        along_x = (column[7].astype(jnp.float32) + steps_f)[None, None, :]
        shift_vec = jnp.stack([jnp.mean(weight * along_z), jnp.mean(weight * along_y), jnp.mean(weight * along_x)]) / (energy + EPSILON)
        center = jnp.stack([
            (slab_pos.astype(jnp.float32) * B + 0.5 * B) / (B * N_SLAB),
            jnp.ones((), jnp.float32) * 0.5,
            (column[1].astype(jnp.float32) + 0.5 * B) / (2.0 * B),
            jnp.ones((), jnp.float32)])
        hit_a = (view_ids == column[0]).astype(jnp.float32)
        hit_b = (view_ids == column[2]).astype(jnp.float32)
        outer_hh = energy * center[:, None] * center[None, :]
        normal_part = (hit_a + hit_b)[:, None, None] * outer_hh[None]
        rhs_part = (hit_a - hit_b)[:, None, None] * (energy * center[:, None] * shift_vec[None, :])[None]
        return values.reshape(-1), shift_vec, normal_part, rhs_part

    corr_rows, shift_rows, normal_parts, rhs_parts = lax.map(one_pair, jnp.arange(pair_total, dtype=jnp.int32))
    normal_sums = jnp.sum(normal_parts, axis=0) / pair_total
    rhs_sums = jnp.sum(rhs_parts, axis=0) / pair_total
    return corr_rows, jnp.transpose(shift_rows), normal_sums, rhs_sums
```

```python
import math

import jax
import jax.numpy as jnp
import numpy as np
from jax import lax
from jax.experimental import pallas as pl
from jax.experimental.pallas import tpu as pltpu
from jax.sharding import PartitionSpec as P

WIN = 8
NBR = 2
EPSILON = 1e-06
GAP = 8
PRECISE = lax.Precision.HIGHEST


def passed_along(value, axis, steps):
    count = lax.axis_size(axis)
    leading, last = (max(0, -steps), min(count, count - steps))
    return lax.ppermute(value, axis, [(source, source + steps) for source in range(leading, last)])


def split(values):
    high = values.astype(jnp.bfloat16)
    return high, (values - high.astype(jnp.float32)).astype(jnp.bfloat16)


def split_outside(values):
    high = lax.reduce_precision(values, 8, 7)
    return high.astype(jnp.bfloat16), (values - high).astype(jnp.bfloat16)


def static_tables(edge):
    ids = np.arange(edge)
    cells = np.arange(2 * edge) % edge
    angles = 2 * np.pi * (np.outer(cells, ids) % edge) / edge
    table_a = np.concatenate([np.cos(angles), -np.sin(angles)], axis=1)
    table_b = np.concatenate([np.sin(angles), np.cos(angles)], axis=1)
    table_x = np.concatenate([table_a, table_b], axis=0).astype(np.float32)
    high = table_x.astype(jnp.bfloat16)
    low = (table_x - high.astype(np.float32)).astype(jnp.bfloat16)
    table_x = np.concatenate([high, low], axis=1).astype(np.float32)
    angles = 2 * np.pi * (np.outer(ids, ids) % edge) / edge
    table_y = np.concatenate([np.cos(angles), np.sin(angles)], axis=0).astype(np.float32)
    high = table_y.astype(jnp.bfloat16)
    low = (table_y - high.astype(np.float32)).astype(jnp.bfloat16)
    return table_x, np.concatenate([high, low, high], axis=1)


def window_tables(fields, edge):
    steps = jnp.arange(WIN, dtype=jnp.int32)
    ids = jnp.arange(edge, dtype=jnp.int32)
    offsets = fields[5:8] + jnp.stack([0 * fields[1], 0 * fields[1], fields[1] - fields[4]])
    product = jnp.mod((offsets[:, :, None] + steps)[..., None] * ids, edge)
    angles = (2.0 * math.pi / edge) * product.astype(jnp.float32)
    cos_all, sin_all = jnp.cos(angles), jnp.sin(angles)
    both = jnp.concatenate([cos_all, sin_all], axis=2)
    high, low = split_outside(both[0])
    table_z = jnp.concatenate([high, low, high], axis=2)
    table_y = jnp.pad(both[1], ((0, 0), (0, 0), (0, edge)))
    table_x = jnp.concatenate([cos_all[2], -sin_all[2]], axis=2) / edge**1.5
    table_x = jnp.pad(table_x, ((0, 0), (0, 2 * edge - WIN), (0, 0)))
    return table_z, table_y, jnp.swapaxes(table_x, 1, 2)


def find_request(fields, count, direction, level):
    seen = jnp.int32(0)
    view, anchor = jnp.int32(0), jnp.int32(0)
    for slot in range(fields.shape[1]):
        wanted = (fields[3, slot] == direction) & (slot < count)
        take = wanted & (seen == level)
        view = jnp.where(take, fields[2, slot], view)
        anchor = jnp.where(take, fields[4, slot], anchor)
        seen = seen + wanted.astype(jnp.int32)
    return view, anchor


def pack_kernel(below_ref, above_ref, volumes_ref, up_ref, down_ref, held, sems):
    edge = up_ref.shape[0]
    picks = []
    for side, (list_ref, direction) in enumerate([(below_ref, 1), (above_ref, -1)]):
        for level in range(NBR):
            picks.append(find_request(list_ref, list_ref[8, 0], direction, level))
    copies = []
    for index, (view, _) in enumerate(picks):
        copy = pltpu.make_async_copy(volumes_ref.at[view], held.at[index], sems.at[index])
        copy.start()
        copies.append(copy)
    for side, out_ref in enumerate([up_ref, down_ref]):
        copies[2 * side].wait()
        copies[2 * side + 1].wait()
        first_x, second_x = picks[2 * side][1], picks[2 * side + 1][1]

        def step(z, _):
            lanes = lax.broadcasted_iota(jnp.int32, (edge, 2 * edge), 1)
            first = held[2 * side, z].astype(jnp.float32)
            second = held[2 * side + 1, z].astype(jnp.float32)
            straight = jnp.where(lanes < edge, first, second)
            turned = pltpu.roll(jnp.where(lanes < edge, second, first), edge, 1)
            keep = ((lanes < edge) & (lanes >= first_x)) | (
                (lanes >= edge) & (lanes < edge + second_x)
            )
            out_ref[z] = jnp.where(keep, straight, turned).astype(jnp.bfloat16)
            return 0

        lax.fori_loop(0, edge, step, 0, unroll=4)


def pack(volumes, below, above):
    edge = volumes.shape[1]
    shape = jax.ShapeDtypeStruct(volumes.shape[1:], volumes.dtype)
    return pl.pallas_call(
        pack_kernel,
        out_shape=(shape, shape),
        in_specs=[
            pl.BlockSpec(memory_space=pltpu.SMEM),
            pl.BlockSpec(memory_space=pltpu.SMEM),
            pl.BlockSpec(memory_space=pl.ANY),
        ],
        out_specs=(
            pl.BlockSpec(memory_space=pltpu.VMEM),
            pl.BlockSpec(memory_space=pltpu.VMEM),
        ),
        scratch_shapes=[
            pltpu.VMEM((4, edge, edge, 2 * edge), volumes.dtype),
            pltpu.SemaphoreType.DMA((4,)),
        ],
        name="pack",
    )(below, above, volumes)


def pair_kernel(
    slab_count,
    pair_total,
    fields_ref,
    counts_ref,
    volumes_ref,
    above_ref,
    below_ref,
    table_x_ref,
    table_y_ref,
    win_z_ref,
    win_y_ref,
    win_x_ref,
    corr_ref,
    shift_ref,
    sums_ref,
    a_buf,
    b_buf,
    sems,
    table_buf,
    y_buf,
    c_buf,
    m_buf,
    g_buf,
):
    edge = volumes_ref.shape[1]
    lanes_all = 2 * edge
    half = edge // 2
    cap = fields_ref.shape[1]
    pitch = edge + GAP
    count = counts_ref[0]
    own_index = lax.axis_index("slab")

    def fetch(slot, start):
        buf = lax.rem(slot, 2)
        copy_a = pltpu.make_async_copy(
            volumes_ref.at[fields_ref[0, slot]], a_buf.at[buf], sems.at[0, buf]
        )
        copy_b = pltpu.make_async_copy(
            volumes_ref.at[fields_ref[2, slot]], b_buf.at[buf], sems.at[1, buf]
        )
        if not start:
            copy_a.wait()
            copy_b.wait()
            return
        copy_a.start()
        direction = fields_ref[3, slot]

        @pl.when(direction == 0)
        def _():
            copy_b.start()

        @pl.when(direction == 1)
        def _():
            pltpu.make_async_copy(above_ref, b_buf.at[buf], sems.at[1, buf]).start()

        @pl.when(direction == -1)
        def _():
            pltpu.make_async_copy(below_ref, b_buf.at[buf], sems.at[1, buf]).start()

    fetch(jnp.int32(0), True)
    corr_ref[...] = jnp.zeros_like(corr_ref)
    shift_ref[...] = jnp.zeros_like(shift_ref)
    sums_ref[...] = jnp.zeros_like(sums_ref)
    c_buf[half + 1] = jnp.zeros((edge, lanes_all), jnp.float32)
    m_buf[half + 1] = jnp.zeros((edge, lanes_all), jnp.float32)

    def pair_step(slot, _):
        buf = lax.rem(slot, 2)

        @pl.when(slot + 1 < count)
        def _():
            fetch(slot + 1, True)

        direction = fields_ref[3, slot]
        rank = jnp.int32(0)
        for other in range(cap):
            rank = rank + ((fields_ref[3, other] == direction) & (other < slot)).astype(jnp.int32)
        start_a = fields_ref[1, slot]
        start_b = jnp.where(direction == 0, fields_ref[4, slot], edge * rank)
        rows = lax.broadcasted_iota(jnp.int32, (lanes_all, 2 * lanes_all), 0)
        for part, start in enumerate((start_a, start_b)):
            where = pl.ds(part * lanes_all, lanes_all)
            inside = (rows >= start) & (rows < start + edge)
            table_buf[where, :] = jnp.where(inside, table_x_ref[where, :], 0.0).astype(jnp.bfloat16)
        fetch(slot, False)

        lanes = lax.broadcasted_iota(jnp.int32, (edge, lanes_all), 1)
        low = lanes < edge
        sign = jnp.where(low, 1.0, -1.0)

        def xy_step(step, _):
            z = 2 * step
            left = a_buf[buf, pl.ds(z, 2)].reshape(2 * edge, lanes_all)
            right = b_buf[buf, pl.ds(z, 2)].reshape(2 * edge, lanes_all)
            mixed = jnp.dot(
                jnp.concatenate([left, right], axis=1),
                table_buf[...],
                preferred_element_type=jnp.float32,
            )
            high, rest = split(mixed[:, :lanes_all] + mixed[:, lanes_all:])
            high = jnp.concatenate([high[:edge], high[edge:]], axis=1)
            rest = jnp.concatenate([rest[:edge], rest[edge:]], axis=1)
            mixed = jnp.dot(
                table_y_ref[...],
                jnp.concatenate([high, high, rest], axis=0),
                preferred_element_type=jnp.float32,
            )
            for part in range(2):
                where = slice(part * lanes_all, (part + 1) * lanes_all)
                turned = pltpu.roll(mixed[edge:, where], edge, 1)
                y_buf[pl.ds(z + part, edge, stride=pitch), :] = mixed[:edge, where] + sign * turned
            return 0

        lax.fori_loop(0, edge // 2, xy_step, 0, unroll=4)

        reversed_ids = jnp.where(low, (edge - lanes) % edge, edge + (lanes_all - lanes) % edge)

        def z_step(ky, total):
            mirror = lax.rem(edge - ky, edge)
            plane = y_buf[pl.ds(pl.multiple_of(ky * pitch, 8), edge), :]
            other = y_buf[pl.ds(pl.multiple_of(mirror * pitch, 8), edge), :]
            high, rest = split(jnp.concatenate([plane, other], axis=1))
            mixed = jnp.dot(
                table_y_ref[...],
                jnp.concatenate([high, high, rest], axis=0),
                preferred_element_type=jnp.float32,
            )
            front = mixed[:edge, :lanes_all] + sign * pltpu.roll(mixed[edge:, :lanes_all], edge, 1)
            back = mixed[:edge, lanes_all:] - sign * pltpu.roll(mixed[edge:, lanes_all:], edge, 1)
            back = jnp.take_along_axis(back, reversed_ids, axis=1)
            first = front * pltpu.roll(back, edge, 1)
            second = 0.5 * (front * front - back * back)
            cross = jnp.where(low, first, second) + pltpu.roll(
                jnp.where(low, second, first), edge, 1
            )
            square = cross * cross
            magnitude = jnp.sqrt(square + pltpu.roll(square, edge, 1))
            c_buf[ky] = cross
            m_buf[ky] = magnitude
            times = jnp.where((ky == 0) | (ky == half), 0.5, 1.0)
            return total + times * magnitude

        total = lax.fori_loop(
            0, half + 1, z_step, jnp.zeros((edge, lanes_all), jnp.float32), unroll=3
        )
        floor = jnp.sum(total) / float(edge**3) + 2.0 * EPSILON

        table_z = win_z_ref[slot]
        sign_w = sign[:WIN]

        def win_step(step, _):
            ratios = []
            for part in range(2):
                ky = 2 * step + part
                times = jnp.where((ky == 0) | (ky == half), 1.0, 2.0)
                ratios.append(times * c_buf[ky] / (m_buf[ky] + floor))
            high, rest = split(jnp.concatenate(ratios, axis=1))
            mixed = jnp.dot(
                table_z,
                jnp.concatenate([high, high, rest], axis=0),
                preferred_element_type=jnp.float32,
            )
            for part in range(2):
                where = slice(part * lanes_all, (part + 1) * lanes_all)
                g_buf[pl.ds(pl.multiple_of((2 * step + part) * WIN, 8), WIN), :] = mixed[
                    :WIN, where
                ] - sign_w * pltpu.roll(mixed[WIN:, where], edge, 1)
            return 0

        lax.fori_loop(0, half // 2 + 1, win_step, 0, unroll=3)

        planes = g_buf.shape[0] // WIN
        partial = jnp.concatenate(
            [g_buf[pl.ds(i, planes, stride=WIN), :] for i in range(WIN)], axis=1
        )
        mixed = jnp.dot(
            win_y_ref[slot][:, :planes],
            partial,
            precision=PRECISE,
            preferred_element_type=jnp.float32,
        )
        blocks = []
        for i in range(WIN):
            where = slice(i * lanes_all, (i + 1) * lanes_all)
            blocks.append(mixed[:WIN, where] - sign_w * pltpu.roll(mixed[WIN:, where], edge, 1))
        values = jnp.dot(
            jnp.concatenate(blocks, axis=0),
            win_x_ref[slot],
            precision=PRECISE,
            preferred_element_type=jnp.float32,
        )
        corr_ref[slot] = values

        weight = values * values
        line = lax.broadcasted_iota(jnp.int32, (WIN * WIN, lanes_all), 0)
        lane = lax.broadcasted_iota(jnp.int32, (WIN * WIN, lanes_all), 1)
        cells = float(WIN**3)
        energy = jnp.sum(weight, keepdims=True) / cells
        places = (line // WIN, line % WIN, lane)
        shifts = [
            (jnp.sum(weight * place.astype(jnp.float32), keepdims=True) / cells
             + energy * fields_ref[5 + axis, slot].astype(jnp.float32))
            / (energy + EPSILON)
            for axis, place in enumerate(places)
        ]
        views = sums_ref.shape[0]
        view = lax.broadcasted_iota(jnp.int32, (views, lanes_all), 0)
        entry = lax.broadcasted_iota(jnp.int32, (views, lanes_all), 1)
        center_z = (own_index.astype(jnp.float32) * edge + 0.5 * edge) / (edge * slab_count)
        center_x = (start_a.astype(jnp.float32) + 0.5 * edge) / (2.0 * edge)

        def center(index):
            return jnp.where(
                index == 0,
                center_z,
                jnp.where(index == 1, 0.5, jnp.where(index == 2, center_x, 1.0)),
            )

        hit_a = (view == fields_ref[0, slot]).astype(jnp.float32)
        hit_b = (view == fields_ref[2, slot]).astype(jnp.float32)
        normal = (hit_a + hit_b) * center(entry // 4) * center(entry % 4)
        after = jnp.maximum(entry - 16, 0)
        which = after % 3
        shift = jnp.where(which == 0, shifts[0], jnp.where(which == 1, shifts[1], shifts[2]))
        rhs = (hit_a - hit_b) * center(after // 3) * shift
        sums_ref[...] += jnp.where(entry < 16, normal, jnp.where(entry < 28, rhs, 0.0)) * (
            energy / pair_total
        )
        spot = lax.broadcasted_iota(jnp.int32, shift_ref.shape, 0)
        column = lax.broadcasted_iota(jnp.int32, shift_ref.shape, 1)
        for axis in range(3):
            shift_ref[...] += jnp.where((spot == axis) & (column == slot), shifts[axis], 0.0)
        return 0

    lax.fori_loop(0, count, pair_step, 0)


def pairs(volumes, from_above, from_below, pair_fields, pair_counts, tables, slab_count):
    view_count, edge = volumes.shape[0], volumes.shape[1]
    cap = pair_fields.shape[1]
    lanes = 2 * edge
    half = edge // 2
    table_x, table_y = static_tables(edge)
    smem = pl.BlockSpec(memory_space=pltpu.SMEM)
    vmem = pl.BlockSpec(memory_space=pltpu.VMEM)
    anywhere = pl.BlockSpec(memory_space=pl.ANY)

    def kernel(*refs):
        pair_kernel(slab_count, float(cap * slab_count), *refs)

    return pl.pallas_call(
        kernel,
        out_shape=(
            jax.ShapeDtypeStruct((cap, WIN * WIN, lanes), jnp.float32),
            jax.ShapeDtypeStruct((8, lanes), jnp.float32),
            jax.ShapeDtypeStruct((view_count, lanes), jnp.float32),
        ),
        in_specs=[smem, smem, anywhere, anywhere, anywhere] + [vmem] * 5,
        out_specs=(vmem, vmem, vmem),
        scratch_shapes=[
            pltpu.VMEM((2, edge, edge, lanes), volumes.dtype),
            pltpu.VMEM((2, edge, edge, lanes), volumes.dtype),
            pltpu.SemaphoreType.DMA((2, 2)),
            pltpu.VMEM((2 * lanes, 2 * lanes), jnp.bfloat16),
            pltpu.VMEM((edge * (edge + GAP), lanes), jnp.float32),
            pltpu.VMEM((half + 2, edge, lanes), jnp.float32),
            pltpu.VMEM((half + 2, edge, lanes), jnp.float32),
            pltpu.VMEM(((half + 2) * WIN, lanes), jnp.float32),
        ],
        compiler_params=pltpu.CompilerParams(vmem_limit_bytes=40 * 2**20),
        name="pairs",
    )(
        pair_fields,
        pair_counts,
        volumes,
        from_above,
        from_below,
        jnp.asarray(table_x),
        jnp.asarray(table_y),
        *tables,
    )


def on_device(volumes, pair_fields, pair_counts):
    cap = pair_fields.shape[1]
    edge = volumes.shape[1]
    slab_count = lax.axis_size("slab")
    listed = jnp.concatenate(
        [pair_fields, jnp.broadcast_to(pair_counts[None, :], (1, cap))], axis=0
    )
    below = passed_along(listed, "slab", 1)
    above = passed_along(listed, "slab", -1)
    tables = window_tables(pair_fields, edge)
    up, down = pack(volumes, below, above)
    from_above = passed_along(up, "slab", -1)
    from_below = passed_along(down, "slab", 1)
    corr, shifts, sums = pairs(
        volumes, from_above, from_below, pair_fields, pair_counts, tables, slab_count
    )
    sums = lax.psum(sums, "slab")
    return (
        corr[:, :, :WIN].reshape(cap, WIN**3),
        shifts[:3, :cap],
        sums[:, :16].reshape(-1, 4, 4),
        sums[:, 16:28].reshape(-1, 4, 3),
    )


def solution(mesh):
    in_specs = (P("tm", "slab", None, None), P(None, ("tm", "slab")), P(("tm", "slab")))
    out_specs = (
        P(("tm", "slab"), None),
        P(None, ("tm", "slab")),
        P("tm", None, None),
        P("tm", None, None),
    )
    return jax.shard_map(
        on_device, mesh=mesh, in_specs=in_specs, out_specs=out_specs, check_vma=False
    )
```

```python
import math

import jax
import jax.numpy as jnp
import numpy as np
from jax import lax
from jax.experimental import pallas as pl
from jax.experimental.pallas import tpu as pltpu
from jax.sharding import PartitionSpec as P

WIN = 8
NBR = 2
EPSILON = 1e-06
GAP = 8
PRECISE = lax.Precision.HIGHEST


def passed_along(value, axis, steps):
    count = lax.axis_size(axis)
    leading, last = (max(0, -steps), min(count, count - steps))
    return lax.ppermute(value, axis, [(source, source + steps) for source in range(leading, last)])


def split(values):
    high = values.astype(jnp.bfloat16)
    return high, (values - high.astype(jnp.float32)).astype(jnp.bfloat16)


def split_outside(values):
    high = lax.reduce_precision(values, 8, 7)
    return high.astype(jnp.bfloat16), (values - high).astype(jnp.bfloat16)


def static_tables(edge):
    ids = np.arange(edge)
    cells = np.arange(2 * edge) % edge
    angles = 2 * np.pi * (np.outer(cells, ids) % edge) / edge
    table_a = np.concatenate([np.cos(angles), -np.sin(angles)], axis=1)
    table_b = np.concatenate([np.sin(angles), np.cos(angles)], axis=1)
    table_x = np.concatenate([table_a, table_b], axis=0).astype(np.float32)
    high = table_x.astype(jnp.bfloat16)
    low = (table_x - high.astype(np.float32)).astype(jnp.bfloat16)
    table_x = np.concatenate([high, low], axis=1).astype(np.float32)
    angles = 2 * np.pi * (np.outer(ids, ids) % edge) / edge
    table_y = np.concatenate([np.cos(angles), np.sin(angles)], axis=0).astype(np.float32)
    high = table_y.astype(jnp.bfloat16)
    low = (table_y - high.astype(np.float32)).astype(jnp.bfloat16)
    return table_x, np.concatenate([high, low, high], axis=1)


def window_tables(fields, edge):
    steps = jnp.arange(WIN, dtype=jnp.int32)
    ids = jnp.arange(edge, dtype=jnp.int32)
    offsets = fields[5:8] + jnp.stack([0 * fields[1], 0 * fields[1], fields[1] - fields[4]])
    product = jnp.mod((offsets[:, :, None] + steps)[..., None] * ids, edge)
    angles = (2.0 * math.pi / edge) * product.astype(jnp.float32)
    cos_all, sin_all = jnp.cos(angles), jnp.sin(angles)
    both = jnp.concatenate([cos_all, sin_all], axis=2)
    high, low = split_outside(both[0])
    table_z = jnp.concatenate([high, low, high], axis=2)
    table_y = jnp.pad(both[1], ((0, 0), (0, 0), (0, edge)))
    table_x = jnp.concatenate([cos_all[2], -sin_all[2]], axis=2) / edge**1.5
    table_x = jnp.pad(table_x, ((0, 0), (0, 2 * edge - WIN), (0, 0)))
    return table_z, table_y, jnp.swapaxes(table_x, 1, 2)


def find_request(fields, count, direction, level):
    seen = jnp.int32(0)
    view, anchor = jnp.int32(0), jnp.int32(0)
    for slot in range(fields.shape[1]):
        wanted = (fields[3, slot] == direction) & (slot < count)
        take = wanted & (seen == level)
        view = jnp.where(take, fields[2, slot], view)
        anchor = jnp.where(take, fields[4, slot], anchor)
        seen = seen + wanted.astype(jnp.int32)
    return view, anchor


def pack_kernel(below_ref, above_ref, volumes_ref, up_ref, down_ref, held, sems):
    edge = up_ref.shape[0]
    picks = []
    for side, (list_ref, direction) in enumerate([(below_ref, 1), (above_ref, -1)]):
        for level in range(NBR):
            picks.append(find_request(list_ref, list_ref[8, 0], direction, level))
    copies = []
    for index, (view, _) in enumerate(picks):
        copy = pltpu.make_async_copy(volumes_ref.at[view], held.at[index], sems.at[index])
        copy.start()
        copies.append(copy)
    for side, out_ref in enumerate([up_ref, down_ref]):
        copies[2 * side].wait()
        copies[2 * side + 1].wait()
        first_x, second_x = picks[2 * side][1], picks[2 * side + 1][1]

        def step(z, _):
            lanes = lax.broadcasted_iota(jnp.int32, (edge, 2 * edge), 1)
            first = held[2 * side, z].astype(jnp.float32)
            second = held[2 * side + 1, z].astype(jnp.float32)
            straight = jnp.where(lanes < edge, first, second)
            turned = pltpu.roll(jnp.where(lanes < edge, second, first), edge, 1)
            keep = ((lanes < edge) & (lanes >= first_x)) | (
                (lanes >= edge) & (lanes < edge + second_x)
            )
            out_ref[z] = jnp.where(keep, straight, turned).astype(jnp.bfloat16)
            return 0

        lax.fori_loop(0, edge, step, 0, unroll=4)


def pack(volumes, below, above):
    edge = volumes.shape[1]
    shape = jax.ShapeDtypeStruct(volumes.shape[1:], volumes.dtype)
    return pl.pallas_call(
        pack_kernel,
        out_shape=(shape, shape),
        in_specs=[
            pl.BlockSpec(memory_space=pltpu.SMEM),
            pl.BlockSpec(memory_space=pltpu.SMEM),
            pl.BlockSpec(memory_space=pl.ANY),
        ],
        out_specs=(
            pl.BlockSpec(memory_space=pltpu.VMEM),
            pl.BlockSpec(memory_space=pltpu.VMEM),
        ),
        scratch_shapes=[
            pltpu.VMEM((4, edge, edge, 2 * edge), volumes.dtype),
            pltpu.SemaphoreType.DMA((4,)),
        ],
        name="pack",
    )(below, above, volumes)


def pair_kernel(
    slab_count,
    pair_total,
    fields_ref,
    counts_ref,
    volumes_ref,
    above_ref,
    below_ref,
    table_x_ref,
    table_y_ref,
    win_z_ref,
    win_y_ref,
    win_x_ref,
    corr_ref,
    shift_ref,
    sums_ref,
    a_buf,
    b_buf,
    sems,
    table_buf,
    y_buf,
    c_buf,
    m_buf,
    g_buf,
):
    edge = volumes_ref.shape[1]
    lanes_all = 2 * edge
    half = edge // 2
    cap = fields_ref.shape[1]
    pitch = edge + GAP
    count = counts_ref[0]
    own_index = lax.axis_index("slab")

    def fetch(slot, start):
        buf = lax.rem(slot, 2)
        copy_a = pltpu.make_async_copy(
            volumes_ref.at[fields_ref[0, slot]], a_buf.at[buf], sems.at[0, buf]
        )
        copy_b = pltpu.make_async_copy(
            volumes_ref.at[fields_ref[2, slot]], b_buf.at[buf], sems.at[1, buf]
        )
        if not start:
            copy_a.wait()
            copy_b.wait()
            return
        copy_a.start()
        direction = fields_ref[3, slot]

        @pl.when(direction == 0)
        def _():
            copy_b.start()

        @pl.when(direction == 1)
        def _():
            pltpu.make_async_copy(above_ref, b_buf.at[buf], sems.at[1, buf]).start()

        @pl.when(direction == -1)
        def _():
            pltpu.make_async_copy(below_ref, b_buf.at[buf], sems.at[1, buf]).start()

    fetch(jnp.int32(0), True)
    corr_ref[...] = jnp.zeros_like(corr_ref)
    shift_ref[...] = jnp.zeros_like(shift_ref)
    sums_ref[...] = jnp.zeros_like(sums_ref)
    c_buf[half + 1] = jnp.zeros((edge, lanes_all), jnp.float32)
    m_buf[half + 1] = jnp.zeros((edge, lanes_all), jnp.float32)

    def pair_step(slot, _):
        buf = lax.rem(slot, 2)

        @pl.when(slot + 1 < count)
        def _():
            fetch(slot + 1, True)

        direction = fields_ref[3, slot]
        rank = jnp.int32(0)
        for other in range(cap):
            rank = rank + ((fields_ref[3, other] == direction) & (other < slot)).astype(jnp.int32)
        start_a = fields_ref[1, slot]
        start_b = jnp.where(direction == 0, fields_ref[4, slot], edge * rank)
        rows = lax.broadcasted_iota(jnp.int32, (lanes_all, 2 * lanes_all), 0)
        for part, start in enumerate((start_a, start_b)):
            where = pl.ds(part * lanes_all, lanes_all)
            inside = (rows >= start) & (rows < start + edge)
            table_buf[where, :] = jnp.where(inside, table_x_ref[where, :], 0.0).astype(jnp.bfloat16)
        fetch(slot, False)

        lanes = lax.broadcasted_iota(jnp.int32, (edge, lanes_all), 1)
        low = lanes < edge
        sign = jnp.where(low, 1.0, -1.0)

        def xy_step(step, _):
            z = 2 * step
            left = a_buf[buf, pl.ds(z, 2)].reshape(2 * edge, lanes_all)
            right = b_buf[buf, pl.ds(z, 2)].reshape(2 * edge, lanes_all)
            mixed = jnp.dot(
                jnp.concatenate([left, right], axis=1),
                table_buf[...],
                preferred_element_type=jnp.float32,
            )
            high, rest = split(mixed[:, :lanes_all] + mixed[:, lanes_all:])
            high = jnp.concatenate([high[:edge], high[edge:]], axis=1)
            rest = jnp.concatenate([rest[:edge], rest[edge:]], axis=1)
            mixed = jnp.dot(
                table_y_ref[...],
                jnp.concatenate([high, high, rest], axis=0),
                preferred_element_type=jnp.float32,
            )
            for part in range(2):
                where = slice(part * lanes_all, (part + 1) * lanes_all)
                turned = pltpu.roll(mixed[edge:, where], edge, 1)
                y_buf[pl.ds(z + part, edge, stride=pitch), :] = mixed[:edge, where] + sign * turned
            return 0

        lax.fori_loop(0, edge // 2, xy_step, 0, unroll=4)

        reversed_ids = jnp.where(low, (edge - lanes) % edge, edge + (lanes_all - lanes) % edge)

        def z_step(ky, total):
            mirror = lax.rem(edge - ky, edge)
            plane = y_buf[pl.ds(pl.multiple_of(ky * pitch, 8), edge), :]
            other = y_buf[pl.ds(pl.multiple_of(mirror * pitch, 8), edge), :]
            high, rest = split(jnp.concatenate([plane, other], axis=1))
            mixed = jnp.dot(
                table_y_ref[...],
                jnp.concatenate([high, high, rest], axis=0),
                preferred_element_type=jnp.float32,
            )
            front = mixed[:edge, :lanes_all] + sign * pltpu.roll(mixed[edge:, :lanes_all], edge, 1)
            back = mixed[:edge, lanes_all:] - sign * pltpu.roll(mixed[edge:, lanes_all:], edge, 1)
            back = jnp.take_along_axis(back, reversed_ids, axis=1)
            first = front * pltpu.roll(back, edge, 1)
            second = 0.5 * (front * front - back * back)
            cross = jnp.where(low, first, second) + pltpu.roll(
                jnp.where(low, second, first), edge, 1
            )
            square = cross * cross
            magnitude = jnp.sqrt(square + pltpu.roll(square, edge, 1))
            c_buf[ky] = cross
            m_buf[ky] = magnitude
            times = jnp.where((ky == 0) | (ky == half), 0.5, 1.0)
            return total + times * magnitude

        total = lax.fori_loop(
            0, half + 1, z_step, jnp.zeros((edge, lanes_all), jnp.float32), unroll=3
        )
        floor = jnp.sum(total) / float(edge**3) + 2.0 * EPSILON

        table_z = win_z_ref[slot]
        sign_w = sign[:WIN]

        def win_step(step, _):
            ratios = []
            for part in range(2):
                ky = 2 * step + part
                times = jnp.where((ky == 0) | (ky == half), 1.0, 2.0)
                ratios.append(times * c_buf[ky] / (m_buf[ky] + floor))
            high, rest = split(jnp.concatenate(ratios, axis=1))
            mixed = jnp.dot(
                table_z,
                jnp.concatenate([high, high, rest], axis=0),
                preferred_element_type=jnp.float32,
            )
            for part in range(2):
                where = slice(part * lanes_all, (part + 1) * lanes_all)
                g_buf[pl.ds(pl.multiple_of((2 * step + part) * WIN, 8), WIN), :] = mixed[
                    :WIN, where
                ] - sign_w * pltpu.roll(mixed[WIN:, where], edge, 1)
            return 0

        lax.fori_loop(0, half // 2 + 1, win_step, 0, unroll=3)

        planes = g_buf.shape[0] // WIN
        partial = jnp.concatenate(
            [g_buf[pl.ds(i, planes, stride=WIN), :] for i in range(WIN)], axis=1
        )
        mixed = jnp.dot(
            win_y_ref[slot][:, :planes],
            partial,
            precision=PRECISE,
            preferred_element_type=jnp.float32,
        )
        blocks = []
        for i in range(WIN):
            where = slice(i * lanes_all, (i + 1) * lanes_all)
            blocks.append(mixed[:WIN, where] - sign_w * pltpu.roll(mixed[WIN:, where], edge, 1))
        values = jnp.dot(
            jnp.concatenate(blocks, axis=0),
            win_x_ref[slot],
            precision=PRECISE,
            preferred_element_type=jnp.float32,
        )
        corr_ref[slot] = values

        weight = values * values
        line = lax.broadcasted_iota(jnp.int32, (WIN * WIN, lanes_all), 0)
        lane = lax.broadcasted_iota(jnp.int32, (WIN * WIN, lanes_all), 1)
        cells = float(WIN**3)
        energy = jnp.sum(weight, keepdims=True) / cells
        places = (line // WIN, line % WIN, lane)
        shifts = [
            (jnp.sum(weight * place.astype(jnp.float32), keepdims=True) / cells
             + energy * fields_ref[5 + axis, slot].astype(jnp.float32))
            / (energy + EPSILON)
            for axis, place in enumerate(places)
        ]
        views = sums_ref.shape[0]
        view = lax.broadcasted_iota(jnp.int32, (views, lanes_all), 0)
        entry = lax.broadcasted_iota(jnp.int32, (views, lanes_all), 1)
        center_z = (own_index.astype(jnp.float32) * edge + 0.5 * edge) / (edge * slab_count)
        center_x = (start_a.astype(jnp.float32) + 0.5 * edge) / (2.0 * edge)

        def center(index):
            return jnp.where(
                index == 0,
                center_z,
                jnp.where(index == 1, 0.5, jnp.where(index == 2, center_x, 1.0)),
            )

        hit_a = (view == fields_ref[0, slot]).astype(jnp.float32)
        hit_b = (view == fields_ref[2, slot]).astype(jnp.float32)
        normal = (hit_a + hit_b) * center(entry // 4) * center(entry % 4)
        after = jnp.maximum(entry - 16, 0)
        which = after % 3
        shift = jnp.where(which == 0, shifts[0], jnp.where(which == 1, shifts[1], shifts[2]))
        rhs = (hit_a - hit_b) * center(after // 3) * shift
        sums_ref[...] += jnp.where(entry < 16, normal, jnp.where(entry < 28, rhs, 0.0)) * (
            energy / pair_total
        )
        spot = lax.broadcasted_iota(jnp.int32, shift_ref.shape, 0)
        column = lax.broadcasted_iota(jnp.int32, shift_ref.shape, 1)
        for axis in range(3):
            shift_ref[...] += jnp.where((spot == axis) & (column == slot), shifts[axis], 0.0)
        return 0

    lax.fori_loop(0, count, pair_step, 0)


def pairs(volumes, from_above, from_below, pair_fields, pair_counts, tables, slab_count):
    view_count, edge = volumes.shape[0], volumes.shape[1]
    cap = pair_fields.shape[1]
    lanes = 2 * edge
    half = edge // 2
    table_x, table_y = static_tables(edge)
    smem = pl.BlockSpec(memory_space=pltpu.SMEM)
    vmem = pl.BlockSpec(memory_space=pltpu.VMEM)
    anywhere = pl.BlockSpec(memory_space=pl.ANY)

    def kernel(*refs):
        pair_kernel(slab_count, float(cap * slab_count), *refs)

    return pl.pallas_call(
        kernel,
        out_shape=(
            jax.ShapeDtypeStruct((cap, WIN * WIN, lanes), jnp.float32),
            jax.ShapeDtypeStruct((8, lanes), jnp.float32),
            jax.ShapeDtypeStruct((view_count, lanes), jnp.float32),
        ),
        in_specs=[smem, smem, anywhere, anywhere, anywhere] + [vmem] * 5,
        out_specs=(vmem, vmem, vmem),
        scratch_shapes=[
            pltpu.VMEM((2, edge, edge, lanes), volumes.dtype),
            pltpu.VMEM((2, edge, edge, lanes), volumes.dtype),
            pltpu.SemaphoreType.DMA((2, 2)),
            pltpu.VMEM((2 * lanes, 2 * lanes), jnp.bfloat16),
            pltpu.VMEM((edge * (edge + GAP), lanes), jnp.float32),
            pltpu.VMEM((half + 2, edge, lanes), jnp.float32),
            pltpu.VMEM((half + 2, edge, lanes), jnp.float32),
            pltpu.VMEM(((half + 2) * WIN, lanes), jnp.float32),
        ],
        compiler_params=pltpu.CompilerParams(vmem_limit_bytes=40 * 2**20),
        name="pairs",
    )(
        pair_fields,
        pair_counts,
        volumes,
        from_above,
        from_below,
        jnp.asarray(table_x),
        jnp.asarray(table_y),
        *tables,
    )


def sum_kernel(part_ref, out_ref, held, send_sems, recv_sems):
    count = lax.axis_size("slab")
    own = lax.axis_index("slab")
    barrier = pltpu.get_barrier_semaphore()
    for step in range(1, count):
        peer = lax.rem(own + step, count)
        pl.semaphore_signal(
            barrier, inc=1, device_id={"slab": peer}, device_id_type=pl.DeviceIdType.MESH
        )
    pl.semaphore_wait(barrier, count - 1)

    def copy_to(peer, source):
        return pltpu.make_async_remote_copy(
            src_ref=part_ref,
            dst_ref=held.at[source],
            send_sem=send_sems.at[peer],
            recv_sem=recv_sems.at[source],
            device_id={"slab": peer},
            device_id_type=pl.DeviceIdType.MESH,
        )

    for step in range(1, count):
        copy_to(lax.rem(own + step, count), own).start()
    held[own] = part_ref[...]
    for step in range(1, count):
        peer = lax.rem(own + step, count)
        copy_to(peer, own).wait_send()
        copy_to(peer, peer).wait_recv()
    total = held[0]
    for index in range(1, count):
        total = total + held[index]
    out_ref[...] = total


def summed(part):
    count = lax.axis_size("slab")
    return pl.pallas_call(
        sum_kernel,
        out_shape=jax.ShapeDtypeStruct(part.shape, part.dtype),
        in_specs=[pl.BlockSpec(memory_space=pltpu.VMEM)],
        out_specs=pl.BlockSpec(memory_space=pltpu.VMEM),
        scratch_shapes=[
            pltpu.VMEM((count,) + part.shape, part.dtype),
            pltpu.SemaphoreType.DMA((count,)),
            pltpu.SemaphoreType.DMA((count,)),
        ],
        compiler_params=pltpu.CompilerParams(collective_id=0, has_side_effects=True),
        name="slab_sum",
    )(part)


def on_device(volumes, pair_fields, pair_counts):
    cap = pair_fields.shape[1]
    edge = volumes.shape[1]
    slab_count = lax.axis_size("slab")
    listed = jnp.concatenate(
        [pair_fields, jnp.broadcast_to(pair_counts[None, :], (1, cap))], axis=0
    )
    below = passed_along(listed, "slab", 1)
    above = passed_along(listed, "slab", -1)
    tables = window_tables(pair_fields, edge)
    up, down = pack(volumes, below, above)
    from_above = passed_along(up, "slab", -1)
    from_below = passed_along(down, "slab", 1)
    corr, shifts, sums = pairs(
        volumes, from_above, from_below, pair_fields, pair_counts, tables, slab_count
    )
    sums = summed(sums)
    return (
        corr[:, :, :WIN].reshape(cap, WIN**3),
        shifts[:3, :cap],
        sums[:, :16].reshape(-1, 4, 4),
        sums[:, 16:28].reshape(-1, 4, 3),
    )


def solution(mesh):
    in_specs = (P("tm", "slab", None, None), P(None, ("tm", "slab")), P(("tm", "slab")))
    out_specs = (
        P(("tm", "slab"), None),
        P(None, ("tm", "slab")),
        P("tm", None, None),
        P("tm", None, None),
    )
    return jax.shard_map(
        on_device, mesh=mesh, in_specs=in_specs, out_specs=out_specs, check_vma=False
    )
```

```python
import math

import jax
import jax.numpy as jnp
import numpy as np
from jax import lax
from jax.experimental import pallas as pl
from jax.experimental.pallas import tpu as pltpu
from jax.sharding import PartitionSpec as P

WIN = 8
NBR = 2
EPSILON = 1e-06
GAP = 8
CHUNK = 16
PRECISE = lax.Precision.HIGHEST


def passed_along(value, axis, steps):
    count = lax.axis_size(axis)
    leading, last = (max(0, -steps), min(count, count - steps))
    return lax.ppermute(value, axis, [(source, source + steps) for source in range(leading, last)])


def split(values):
    high = values.astype(jnp.bfloat16)
    return high, (values - high.astype(jnp.float32)).astype(jnp.bfloat16)


def split_outside(values):
    high = lax.reduce_precision(values, 8, 7)
    return high.astype(jnp.bfloat16), (values - high).astype(jnp.bfloat16)


def static_tables(edge):
    ids = np.arange(edge)
    cells = np.arange(2 * edge) % edge
    angles = 2 * np.pi * (np.outer(cells, ids) % edge) / edge
    table_a = np.concatenate([np.cos(angles), -np.sin(angles)], axis=1)
    table_b = np.concatenate([np.sin(angles), np.cos(angles)], axis=1)
    table_x = np.concatenate([table_a, table_b], axis=0).astype(np.float32)
    high = table_x.astype(jnp.bfloat16)
    low = (table_x - high.astype(np.float32)).astype(jnp.bfloat16)
    table_x = np.concatenate([high, low], axis=1).astype(np.float32)
    angles = 2 * np.pi * (np.outer(ids, ids) % edge) / edge
    table_y = np.concatenate([np.cos(angles), np.sin(angles)], axis=0).astype(np.float32)
    high = table_y.astype(jnp.bfloat16)
    low = (table_y - high.astype(np.float32)).astype(jnp.bfloat16)
    return table_x, np.concatenate([high, low, high], axis=1)


def window_tables(fields, edge):
    steps = jnp.arange(WIN, dtype=jnp.int32)
    ids = jnp.arange(edge, dtype=jnp.int32)
    offsets = fields[5:8] + jnp.stack([0 * fields[1], 0 * fields[1], fields[1] - fields[4]])
    product = jnp.mod((offsets[:, :, None] + steps)[..., None] * ids, edge)
    angles = (2.0 * math.pi / edge) * product.astype(jnp.float32)
    cos_all, sin_all = jnp.cos(angles), jnp.sin(angles)
    both = jnp.concatenate([cos_all, sin_all], axis=2)
    high, low = split_outside(both[0])
    table_z = jnp.concatenate([high, low, high], axis=2)
    table_y = jnp.pad(both[1], ((0, 0), (0, 0), (0, edge)))
    table_x = jnp.concatenate([cos_all[2], -sin_all[2]], axis=2) / edge**1.5
    table_x = jnp.pad(table_x, ((0, 0), (0, 2 * edge - WIN), (0, 0)))
    return table_z, table_y, jnp.swapaxes(table_x, 1, 2)


def find_request(fields, count, direction, level):
    seen = jnp.int32(0)
    view, anchor = jnp.int32(0), jnp.int32(0)
    for slot in range(fields.shape[1]):
        wanted = (fields[3, slot] == direction) & (slot < count)
        take = wanted & (seen == level)
        view = jnp.where(take, fields[2, slot], view)
        anchor = jnp.where(take, fields[4, slot], anchor)
        seen = seen + wanted.astype(jnp.int32)
    return view, anchor


def pack_kernel(below_ref, above_ref, volumes_ref, up_ref, down_ref, held, sems):
    edge = up_ref.shape[0]
    picks = []
    for side, (list_ref, direction) in enumerate([(below_ref, 1), (above_ref, -1)]):
        for level in range(NBR):
            picks.append(find_request(list_ref, list_ref[8, 0], direction, level))
    copies = []
    for index, (view, _) in enumerate(picks):
        copy = pltpu.make_async_copy(volumes_ref.at[view], held.at[index], sems.at[index])
        copy.start()
        copies.append(copy)
    for side, out_ref in enumerate([up_ref, down_ref]):
        copies[2 * side].wait()
        copies[2 * side + 1].wait()
        first_x, second_x = picks[2 * side][1], picks[2 * side + 1][1]

        def step(z, _):
            lanes = lax.broadcasted_iota(jnp.int32, (edge, 2 * edge), 1)
            first = held[2 * side, z].astype(jnp.float32)
            second = held[2 * side + 1, z].astype(jnp.float32)
            straight = jnp.where(lanes < edge, first, second)
            turned = pltpu.roll(jnp.where(lanes < edge, second, first), edge, 1)
            keep = ((lanes < edge) & (lanes >= first_x)) | (
                (lanes >= edge) & (lanes < edge + second_x)
            )
            out_ref[z] = jnp.where(keep, straight, turned).astype(jnp.bfloat16)
            return 0

        lax.fori_loop(0, edge, step, 0, unroll=4)


def pack(volumes, below, above):
    edge = volumes.shape[1]
    shape = jax.ShapeDtypeStruct(volumes.shape[1:], volumes.dtype)
    return pl.pallas_call(
        pack_kernel,
        out_shape=(shape, shape),
        in_specs=[
            pl.BlockSpec(memory_space=pltpu.SMEM),
            pl.BlockSpec(memory_space=pltpu.SMEM),
            pl.BlockSpec(memory_space=pl.ANY),
        ],
        out_specs=(
            pl.BlockSpec(memory_space=pltpu.VMEM),
            pl.BlockSpec(memory_space=pltpu.VMEM),
        ),
        scratch_shapes=[
            pltpu.VMEM((4, edge, edge, 2 * edge), volumes.dtype),
            pltpu.SemaphoreType.DMA((4,)),
        ],
        name="pack",
    )(below, above, volumes)


def pair_kernel(
    slab_count,
    pair_total,
    fields_ref,
    counts_ref,
    volumes_ref,
    above_ref,
    below_ref,
    table_x_ref,
    table_y_ref,
    win_z_ref,
    win_y_ref,
    win_x_ref,
    corr_ref,
    shift_ref,
    sums_ref,
    a_buf,
    b_buf,
    sems,
    table_buf,
    y_buf,
    c_buf,
    m_buf,
    g_buf,
):
    edge = volumes_ref.shape[1]
    lanes_all = 2 * edge
    half = edge // 2
    cap = fields_ref.shape[1]
    pitch = edge + GAP
    count = counts_ref[0]
    own_index = lax.axis_index("slab")

    def fetch(slot, start):
        buf = lax.rem(slot, 2)
        copy_a = pltpu.make_async_copy(
            volumes_ref.at[fields_ref[0, slot]], a_buf.at[buf], sems.at[0, buf]
        )
        copy_b = pltpu.make_async_copy(
            volumes_ref.at[fields_ref[2, slot]], b_buf.at[buf], sems.at[1, buf]
        )
        if not start:
            copy_a.wait()
            copy_b.wait()
            return
        copy_a.start()
        direction = fields_ref[3, slot]

        @pl.when(direction == 0)
        def _():
            copy_b.start()

        @pl.when(direction == 1)
        def _():
            pltpu.make_async_copy(above_ref, b_buf.at[buf], sems.at[1, buf]).start()

        @pl.when(direction == -1)
        def _():
            pltpu.make_async_copy(below_ref, b_buf.at[buf], sems.at[1, buf]).start()

    fetch(jnp.int32(0), True)
    corr_ref[...] = jnp.zeros_like(corr_ref)
    shift_ref[...] = jnp.zeros_like(shift_ref)
    sums_ref[...] = jnp.zeros_like(sums_ref)
    c_buf[half + 1] = jnp.zeros((edge, lanes_all), jnp.float32)
    m_buf[half + 1] = jnp.zeros((edge, lanes_all), jnp.float32)

    def pair_step(slot, _):
        buf = lax.rem(slot, 2)

        @pl.when(slot + 1 < count)
        def _():
            fetch(slot + 1, True)

        direction = fields_ref[3, slot]
        rank = jnp.int32(0)
        for other in range(cap):
            rank = rank + ((fields_ref[3, other] == direction) & (other < slot)).astype(jnp.int32)
        start_a = fields_ref[1, slot]
        start_b = jnp.where(direction == 0, fields_ref[4, slot], edge * rank)
        rows = lax.broadcasted_iota(jnp.int32, (lanes_all, 2 * lanes_all), 0)
        for part, start in enumerate((start_a, start_b)):
            where = pl.ds(part * lanes_all, lanes_all)
            inside = (rows >= start) & (rows < start + edge)
            table_buf[where, :] = jnp.where(inside, table_x_ref[where, :], 0.0).astype(jnp.bfloat16)
        fetch(slot, False)

        lanes = lax.broadcasted_iota(jnp.int32, (edge, lanes_all), 1)
        low = lanes < edge
        sign = jnp.where(low, 1.0, -1.0)

        def xy_step(step, _):
            z = CHUNK * step
            left = a_buf[buf, pl.ds(z, CHUNK)].reshape(CHUNK * edge, lanes_all)
            right = b_buf[buf, pl.ds(z, CHUNK)].reshape(CHUNK * edge, lanes_all)
            mixed = jnp.dot(
                jnp.concatenate([left, right], axis=1),
                table_buf[...],
                preferred_element_type=jnp.float32,
            )
            high, rest = split(mixed[:, :lanes_all] + mixed[:, lanes_all:])
            high = jnp.concatenate([high[k * edge : (k + 1) * edge] for k in range(CHUNK)], axis=1)
            rest = jnp.concatenate([rest[k * edge : (k + 1) * edge] for k in range(CHUNK)], axis=1)
            mixed = jnp.dot(
                table_y_ref[...],
                jnp.concatenate([high, high, rest], axis=0),
                preferred_element_type=jnp.float32,
            )
            for part in range(CHUNK):
                where = slice(part * lanes_all, (part + 1) * lanes_all)
                turned = pltpu.roll(mixed[edge:, where], edge, 1)
                y_buf[pl.ds(z + part, edge, stride=pitch), :] = mixed[:edge, where] + sign * turned
            return 0

        lax.fori_loop(0, edge // CHUNK, xy_step, 0, unroll=True)

        reversed_ids = jnp.where(low, (edge - lanes) % edge, edge + (lanes_all - lanes) % edge)

        def z_step(ky, total):
            mirror = lax.rem(edge - ky, edge)
            plane = y_buf[pl.ds(pl.multiple_of(ky * pitch, 8), edge), :]
            other = y_buf[pl.ds(pl.multiple_of(mirror * pitch, 8), edge), :]
            high, rest = split(jnp.concatenate([plane, other], axis=1))
            mixed = jnp.dot(
                table_y_ref[...],
                jnp.concatenate([high, high, rest], axis=0),
                preferred_element_type=jnp.float32,
            )
            front = mixed[:edge, :lanes_all] + sign * pltpu.roll(mixed[edge:, :lanes_all], edge, 1)
            back = mixed[:edge, lanes_all:] - sign * pltpu.roll(mixed[edge:, lanes_all:], edge, 1)
            back = jnp.take_along_axis(back, reversed_ids, axis=1)
            first = front * pltpu.roll(back, edge, 1)
            second = 0.5 * (front * front - back * back)
            cross = jnp.where(low, first, second) + pltpu.roll(
                jnp.where(low, second, first), edge, 1
            )
            square = cross * cross
            magnitude = jnp.sqrt(square + pltpu.roll(square, edge, 1))
            c_buf[ky] = cross
            m_buf[ky] = magnitude
            times = jnp.where((ky == 0) | (ky == half), 0.5, 1.0)
            return total + times * magnitude

        total = lax.fori_loop(
            0, half + 1, z_step, jnp.zeros((edge, lanes_all), jnp.float32), unroll=True
        )
        floor = jnp.sum(total) / float(edge**3) + 2.0 * EPSILON

        table_z = win_z_ref[slot]
        sign_w = sign[:WIN]

        def win_step(step, _):
            ratios = []
            for part in range(2):
                ky = 2 * step + part
                times = jnp.where((ky == 0) | (ky == half), 1.0, 2.0)
                ratios.append(times * c_buf[ky] / (m_buf[ky] + floor))
            high, rest = split(jnp.concatenate(ratios, axis=1))
            mixed = jnp.dot(
                table_z,
                jnp.concatenate([high, high, rest], axis=0),
                preferred_element_type=jnp.float32,
            )
            for part in range(2):
                where = slice(part * lanes_all, (part + 1) * lanes_all)
                g_buf[pl.ds(pl.multiple_of((2 * step + part) * WIN, 8), WIN), :] = mixed[
                    :WIN, where
                ] - sign_w * pltpu.roll(mixed[WIN:, where], edge, 1)
            return 0

        lax.fori_loop(0, half // 2 + 1, win_step, 0, unroll=True)

        planes = g_buf.shape[0] // WIN
        partial = jnp.concatenate(
            [g_buf[pl.ds(i, planes, stride=WIN), :] for i in range(WIN)], axis=1
        )
        mixed = jnp.dot(
            win_y_ref[slot][:, :planes],
            partial,
            precision=PRECISE,
            preferred_element_type=jnp.float32,
        )
        blocks = []
        for i in range(WIN):
            where = slice(i * lanes_all, (i + 1) * lanes_all)
            blocks.append(mixed[:WIN, where] - sign_w * pltpu.roll(mixed[WIN:, where], edge, 1))
        values = jnp.dot(
            jnp.concatenate(blocks, axis=0),
            win_x_ref[slot],
            precision=PRECISE,
            preferred_element_type=jnp.float32,
        )
        corr_ref[slot] = values

        weight = values * values
        line = lax.broadcasted_iota(jnp.int32, (WIN * WIN, lanes_all), 0)
        lane = lax.broadcasted_iota(jnp.int32, (WIN * WIN, lanes_all), 1)
        cells = float(WIN**3)
        energy = jnp.sum(weight, keepdims=True) / cells
        places = (line // WIN, line % WIN, lane)
        shifts = [
            (jnp.sum(weight * place.astype(jnp.float32), keepdims=True) / cells
             + energy * fields_ref[5 + axis, slot].astype(jnp.float32))
            / (energy + EPSILON)
            for axis, place in enumerate(places)
        ]
        views = sums_ref.shape[0]
        view = lax.broadcasted_iota(jnp.int32, (views, lanes_all), 0)
        entry = lax.broadcasted_iota(jnp.int32, (views, lanes_all), 1)
        center_z = (own_index.astype(jnp.float32) * edge + 0.5 * edge) / (edge * slab_count)
        center_x = (start_a.astype(jnp.float32) + 0.5 * edge) / (2.0 * edge)

        def center(index):
            return jnp.where(
                index == 0,
                center_z,
                jnp.where(index == 1, 0.5, jnp.where(index == 2, center_x, 1.0)),
            )

        hit_a = (view == fields_ref[0, slot]).astype(jnp.float32)
        hit_b = (view == fields_ref[2, slot]).astype(jnp.float32)
        normal = (hit_a + hit_b) * center(entry // 4) * center(entry % 4)
        after = jnp.maximum(entry - 16, 0)
        which = after % 3
        shift = jnp.where(which == 0, shifts[0], jnp.where(which == 1, shifts[1], shifts[2]))
        rhs = (hit_a - hit_b) * center(after // 3) * shift
        sums_ref[...] += jnp.where(entry < 16, normal, jnp.where(entry < 28, rhs, 0.0)) * (
            energy / pair_total
        )
        spot = lax.broadcasted_iota(jnp.int32, shift_ref.shape, 0)
        column = lax.broadcasted_iota(jnp.int32, shift_ref.shape, 1)
        for axis in range(3):
            shift_ref[...] += jnp.where((spot == axis) & (column == slot), shifts[axis], 0.0)
        return 0

    lax.fori_loop(0, count, pair_step, 0)


def pairs(volumes, from_above, from_below, pair_fields, pair_counts, tables, slab_count):
    view_count, edge = volumes.shape[0], volumes.shape[1]
    cap = pair_fields.shape[1]
    lanes = 2 * edge
    half = edge // 2
    table_x, table_y = static_tables(edge)
    smem = pl.BlockSpec(memory_space=pltpu.SMEM)
    vmem = pl.BlockSpec(memory_space=pltpu.VMEM)
    anywhere = pl.BlockSpec(memory_space=pl.ANY)

    def kernel(*refs):
        pair_kernel(slab_count, float(cap * slab_count), *refs)

    return pl.pallas_call(
        kernel,
        out_shape=(
            jax.ShapeDtypeStruct((cap, WIN * WIN, lanes), jnp.float32),
            jax.ShapeDtypeStruct((8, lanes), jnp.float32),
            jax.ShapeDtypeStruct((view_count, lanes), jnp.float32),
        ),
        in_specs=[smem, smem, anywhere, anywhere, anywhere] + [vmem] * 5,
        out_specs=(vmem, vmem, vmem),
        scratch_shapes=[
            pltpu.VMEM((2, edge, edge, lanes), volumes.dtype),
            pltpu.VMEM((2, edge, edge, lanes), volumes.dtype),
            pltpu.SemaphoreType.DMA((2, 2)),
            pltpu.VMEM((2 * lanes, 2 * lanes), jnp.bfloat16),
            pltpu.VMEM((edge * (edge + GAP), lanes), jnp.float32),
            pltpu.VMEM((half + 2, edge, lanes), jnp.float32),
            pltpu.VMEM((half + 2, edge, lanes), jnp.float32),
            pltpu.VMEM(((half + 2) * WIN, lanes), jnp.float32),
        ],
        compiler_params=pltpu.CompilerParams(vmem_limit_bytes=40 * 2**20),
        name="pairs",
    )(
        pair_fields,
        pair_counts,
        volumes,
        from_above,
        from_below,
        jnp.asarray(table_x),
        jnp.asarray(table_y),
        *tables,
    )


def sum_kernel(part_ref, out_ref, held, send_sems, recv_sems):
    count = lax.axis_size("slab")
    own = lax.axis_index("slab")
    barrier = pltpu.get_barrier_semaphore()
    for step in range(1, count):
        peer = lax.rem(own + step, count)
        pl.semaphore_signal(
            barrier, inc=1, device_id={"slab": peer}, device_id_type=pl.DeviceIdType.MESH
        )
    pl.semaphore_wait(barrier, count - 1)

    def copy_to(peer, source):
        return pltpu.make_async_remote_copy(
            src_ref=part_ref,
            dst_ref=held.at[source],
            send_sem=send_sems.at[peer],
            recv_sem=recv_sems.at[source],
            device_id={"slab": peer},
            device_id_type=pl.DeviceIdType.MESH,
        )

    for step in range(1, count):
        copy_to(lax.rem(own + step, count), own).start()
    held[own] = part_ref[...]
    for step in range(1, count):
        peer = lax.rem(own + step, count)
        copy_to(peer, own).wait_send()
        copy_to(peer, peer).wait_recv()
    total = held[0]
    for index in range(1, count):
        total = total + held[index]
    out_ref[...] = total


def summed(part):
    count = lax.axis_size("slab")
    return pl.pallas_call(
        sum_kernel,
        out_shape=jax.ShapeDtypeStruct(part.shape, part.dtype),
        in_specs=[pl.BlockSpec(memory_space=pltpu.VMEM)],
        out_specs=pl.BlockSpec(memory_space=pltpu.VMEM),
        scratch_shapes=[
            pltpu.VMEM((count,) + part.shape, part.dtype),
            pltpu.SemaphoreType.DMA((count,)),
            pltpu.SemaphoreType.DMA((count,)),
        ],
        compiler_params=pltpu.CompilerParams(collective_id=0, has_side_effects=True),
        name="slab_sum",
    )(part)


def on_device(volumes, pair_fields, pair_counts):
    cap = pair_fields.shape[1]
    edge = volumes.shape[1]
    slab_count = lax.axis_size("slab")
    listed = jnp.concatenate(
        [pair_fields, jnp.broadcast_to(pair_counts[None, :], (1, cap))], axis=0
    )
    below = passed_along(listed, "slab", 1)
    above = passed_along(listed, "slab", -1)
    tables = window_tables(pair_fields, edge)
    up, down = pack(volumes, below, above)
    from_above = passed_along(up, "slab", -1)
    from_below = passed_along(down, "slab", 1)
    corr, shifts, sums = pairs(
        volumes, from_above, from_below, pair_fields, pair_counts, tables, slab_count
    )
    sums = summed(sums)
    return (
        corr[:, :, :WIN].reshape(cap, WIN**3),
        shifts[:3, :cap],
        sums[:, :16].reshape(-1, 4, 4),
        sums[:, 16:28].reshape(-1, 4, 3),
    )


def solution(mesh):
    in_specs = (P("tm", "slab", None, None), P(None, ("tm", "slab")), P(("tm", "slab")))
    out_specs = (
        P(("tm", "slab"), None),
        P(None, ("tm", "slab")),
        P("tm", None, None),
        P("tm", None, None),
    )
    return jax.shard_map(
        on_device, mesh=mesh, in_specs=in_specs, out_specs=out_specs, check_vma=False
    )
```

```python
import functools
import math

import jax
import jax.numpy as jnp
import numpy as np
from jax import lax
from jax.experimental import pallas as pl
from jax.experimental.pallas import tpu as pltpu
from jax.sharding import PartitionSpec as P

WIN = 8
NBR = 2
EPSILON = 1e-06
GAP = 8
PIECES = 4
CHUNK = 16
PRECISE = lax.Precision.HIGHEST


def split(values):
    high = values.astype(jnp.bfloat16)
    return high, (values - high.astype(jnp.float32)).astype(jnp.bfloat16)


def split_outside(values):
    high = lax.reduce_precision(values, 8, 7)
    return high.astype(jnp.bfloat16), (values - high).astype(jnp.bfloat16)


def static_tables(edge):
    ids = np.arange(edge)
    cells = np.arange(2 * edge) % edge
    angles = 2 * np.pi * (np.outer(cells, ids) % edge) / edge
    table_a = np.concatenate([np.cos(angles), -np.sin(angles)], axis=1)
    table_b = np.concatenate([np.sin(angles), np.cos(angles)], axis=1)
    table_x = np.concatenate([table_a, table_b], axis=0).astype(np.float32)
    high = table_x.astype(jnp.bfloat16)
    low = (table_x - high.astype(np.float32)).astype(jnp.bfloat16)
    table_x = np.concatenate([high, low], axis=1).astype(np.float32)
    angles = 2 * np.pi * (np.outer(ids, ids) % edge) / edge
    table_y = np.concatenate([np.cos(angles), np.sin(angles)], axis=0).astype(np.float32)
    high = table_y.astype(jnp.bfloat16)
    low = (table_y - high.astype(np.float32)).astype(jnp.bfloat16)
    return table_x, np.concatenate([high, low, high], axis=1)


def window_tables(fields, edge):
    steps = jnp.arange(WIN, dtype=jnp.int32)
    ids = jnp.arange(edge, dtype=jnp.int32)
    offsets = fields[5:8] + jnp.stack([0 * fields[1], 0 * fields[1], fields[1] - fields[4]])
    product = jnp.mod((offsets[:, :, None] + steps)[..., None] * ids, edge)
    angles = (2.0 * math.pi / edge) * product.astype(jnp.float32)
    cos_all, sin_all = jnp.cos(angles), jnp.sin(angles)
    both = jnp.concatenate([cos_all, sin_all], axis=2)
    high, low = split_outside(both[0])
    table_z = jnp.concatenate([high, low, high], axis=2)
    table_y = jnp.pad(both[1], ((0, 0), (0, 0), (0, edge)))
    table_x = jnp.concatenate([cos_all[2], -sin_all[2]], axis=2) / edge**1.5
    table_x = jnp.pad(table_x, ((0, 0), (0, 2 * edge - WIN), (0, 0)))
    return table_z, table_y, jnp.swapaxes(table_x, 1, 2)


def find_request(fields, slots, direction, level):
    seen = jnp.int32(0)
    view, anchor = jnp.int32(0), jnp.int32(0)
    for slot in range(slots):
        wanted = fields[3, slot] == direction
        take = wanted & (seen == level)
        view = jnp.where(take, fields[2, slot], view)
        anchor = jnp.where(take, fields[4, slot], anchor)
        seen = seen + wanted.astype(jnp.int32)
    return view, anchor


def exchange_kernel(
    slots,
    list_ref,
    volumes_ref,
    above_ref,
    below_ref,
    held,
    list_in,
    list_smem,
    packed,
    local_sems,
    list_send,
    list_recv,
    send_sems,
    recv_sems,
):
    edge = above_ref.shape[0]
    cells = edge // PIECES
    count = lax.axis_size("slab")
    own = lax.axis_index("slab")
    load = pltpu.make_async_copy(volumes_ref, held, local_sems.at[0])
    load.start()
    list_in[...] = jnp.zeros_like(list_in)
    present = (own > 0, own < count - 1)
    peers = (lax.rem(own + count - 1, count), lax.rem(own + 1, count))
    results = (above_ref, below_ref)
    barrier = pltpu.get_barrier_semaphore()

    def on(side, action):
        pl.when(present[side])(action)

    for side in range(2):
        on(
            side,
            lambda side=side: pl.semaphore_signal(
                barrier,
                inc=1,
                device_id={"slab": peers[side]},
                device_id_type=pl.DeviceIdType.MESH,
            ),
        )
    pl.semaphore_wait(barrier, present[0].astype(jnp.int32) + present[1].astype(jnp.int32))

    def list_copy(side):
        return pltpu.make_async_remote_copy(
            src_ref=list_ref,
            dst_ref=list_in.at[1 - side],
            send_sem=list_send.at[side],
            recv_sem=list_recv.at[1 - side],
            device_id={"slab": peers[side]},
            device_id_type=pl.DeviceIdType.MESH,
        )

    def list_arrival(side):
        return pltpu.make_async_remote_copy(
            src_ref=list_ref,
            dst_ref=list_in.at[side],
            send_sem=list_send.at[side],
            recv_sem=list_recv.at[side],
            device_id={"slab": peers[side]},
            device_id_type=pl.DeviceIdType.MESH,
        )

    for side in range(2):
        on(side, lambda side=side: list_copy(side).start())
    for side in range(2):
        on(side, lambda side=side: list_arrival(side).wait_recv())
    to_smem = pltpu.make_async_copy(list_in, list_smem, local_sems.at[1])
    to_smem.start()
    to_smem.wait()
    picks = []
    for side, direction in enumerate((1, -1)):
        picks.append(
            [find_request(list_smem.at[side], slots, direction, level) for level in range(NBR)]
        )
    load.wait()

    def pack_piece(side, piece):
        (first_view, first_x), (second_view, second_x) = picks[side]

        def step(index, _):
            z = piece * cells + index
            lanes = lax.broadcasted_iota(jnp.int32, (edge, 2 * edge), 1)
            first = held[first_view, z].astype(jnp.float32)
            second = held[second_view, z].astype(jnp.float32)
            straight = jnp.where(lanes < edge, first, second)
            turned = pltpu.roll(jnp.where(lanes < edge, second, first), edge, 1)
            keep = ((lanes < edge) & (lanes >= first_x)) | (
                (lanes >= edge) & (lanes < edge + second_x)
            )
            packed[side, z] = jnp.where(keep, straight, turned).astype(jnp.bfloat16)
            return 0

        lax.fori_loop(0, cells, step, 0, unroll=8)

    def window_copy(side, piece):
        where = pl.ds(piece * cells, cells)
        return pltpu.make_async_remote_copy(
            src_ref=packed.at[side, where],
            dst_ref=results[side].at[where],
            send_sem=send_sems.at[side, piece],
            recv_sem=recv_sems.at[side, piece],
            device_id={"slab": peers[side]},
            device_id_type=pl.DeviceIdType.MESH,
        )

    def window_arrival(side, piece):
        where = pl.ds(piece * cells, cells)
        return pltpu.make_async_remote_copy(
            src_ref=packed.at[side, where],
            dst_ref=results[1 - side].at[where],
            send_sem=send_sems.at[side, piece],
            recv_sem=recv_sems.at[1 - side, piece],
            device_id={"slab": peers[side]},
            device_id_type=pl.DeviceIdType.MESH,
        )

    items = [(side, piece) for piece in range(PIECES) for side in range(2)]
    for number, (side, piece) in enumerate(items):
        pack_piece(side, piece)
        if number:
            previous = items[number - 1]
            on(previous[0], lambda previous=previous: window_copy(*previous).start())
    on(items[-1][0], lambda: window_copy(*items[-1]).start())
    for item in items:
        on(item[0], lambda item=item: window_arrival(*item).wait_recv())
    for item in items:
        on(item[0], lambda item=item: window_copy(*item).wait_send())
    for side in range(2):
        on(side, lambda side=side: list_copy(side).wait_send())


def exchanged(volumes, listed, slots):
    edge = volumes.shape[1]
    shape = jax.ShapeDtypeStruct(volumes.shape[1:], volumes.dtype)
    vmem = pl.BlockSpec(memory_space=pltpu.VMEM)
    return pl.pallas_call(
        functools.partial(exchange_kernel, slots),
        out_shape=(shape, shape),
        in_specs=[vmem, pl.BlockSpec(memory_space=pltpu.HBM)],
        out_specs=(vmem, vmem),
        scratch_shapes=[
            pltpu.VMEM(volumes.shape, volumes.dtype),
            pltpu.VMEM((2,) + listed.shape, listed.dtype),
            pltpu.SMEM((2,) + listed.shape, listed.dtype),
            pltpu.VMEM((2,) + volumes.shape[1:], volumes.dtype),
            pltpu.SemaphoreType.DMA((2,)),
            pltpu.SemaphoreType.DMA((2,)),
            pltpu.SemaphoreType.DMA((2,)),
            pltpu.SemaphoreType.DMA((2, PIECES)),
            pltpu.SemaphoreType.DMA((2, PIECES)),
        ],
        compiler_params=pltpu.CompilerParams(
            collective_id=1, has_side_effects=True, vmem_limit_bytes=24 * 2**20
        ),
        name="exchange",
    )(listed, volumes)


def pair_kernel(
    slab_count,
    pair_total,
    fields_ref,
    counts_ref,
    volumes_ref,
    above_ref,
    below_ref,
    table_x_ref,
    table_y_ref,
    win_z_ref,
    win_y_ref,
    win_x_ref,
    corr_ref,
    shift_ref,
    sums_ref,
    a_buf,
    b_buf,
    sems,
    table_buf,
    y_buf,
    c_buf,
    m_buf,
    g_buf,
):
    edge = volumes_ref.shape[1]
    lanes_all = 2 * edge
    half = edge // 2
    cap = fields_ref.shape[1]
    pitch = edge + GAP
    count = counts_ref[0]
    own_index = lax.axis_index("slab")

    def fetch(slot, start):
        buf = lax.rem(slot, 2)
        copy_a = pltpu.make_async_copy(
            volumes_ref.at[fields_ref[0, slot]], a_buf.at[buf], sems.at[0, buf]
        )
        copy_b = pltpu.make_async_copy(
            volumes_ref.at[fields_ref[2, slot]], b_buf.at[buf], sems.at[1, buf]
        )
        if not start:
            copy_a.wait()
            copy_b.wait()
            return
        copy_a.start()
        direction = fields_ref[3, slot]

        @pl.when(direction == 0)
        def _():
            copy_b.start()

        @pl.when(direction == 1)
        def _():
            pltpu.make_async_copy(above_ref, b_buf.at[buf], sems.at[1, buf]).start()

        @pl.when(direction == -1)
        def _():
            pltpu.make_async_copy(below_ref, b_buf.at[buf], sems.at[1, buf]).start()

    fetch(jnp.int32(0), True)
    corr_ref[...] = jnp.zeros_like(corr_ref)
    shift_ref[...] = jnp.zeros_like(shift_ref)
    sums_ref[...] = jnp.zeros_like(sums_ref)
    c_buf[half + 1] = jnp.zeros((edge, lanes_all), jnp.float32)
    m_buf[half + 1] = jnp.zeros((edge, lanes_all), jnp.float32)

    def pair_step(slot, _):
        buf = lax.rem(slot, 2)

        @pl.when(slot + 1 < count)
        def _():
            fetch(slot + 1, True)

        direction = fields_ref[3, slot]
        rank = jnp.int32(0)
        for other in range(cap):
            rank = rank + ((fields_ref[3, other] == direction) & (other < slot)).astype(jnp.int32)
        start_a = fields_ref[1, slot]
        start_b = jnp.where(direction == 0, fields_ref[4, slot], edge * rank)
        rows = lax.broadcasted_iota(jnp.int32, (lanes_all, 2 * lanes_all), 0)
        for part, start in enumerate((start_a, start_b)):
            where = pl.ds(part * lanes_all, lanes_all)
            inside = (rows >= start) & (rows < start + edge)
            table_buf[where, :] = jnp.where(inside, table_x_ref[where, :], 0.0).astype(jnp.bfloat16)
        fetch(slot, False)

        lanes = lax.broadcasted_iota(jnp.int32, (edge, lanes_all), 1)
        low = lanes < edge
        sign = jnp.where(low, 1.0, -1.0)

        def xy_step(step, _):
            z = CHUNK * step
            left = a_buf[buf, pl.ds(z, CHUNK)].reshape(CHUNK * edge, lanes_all)
            right = b_buf[buf, pl.ds(z, CHUNK)].reshape(CHUNK * edge, lanes_all)
            mixed = jnp.dot(
                jnp.concatenate([left, right], axis=1),
                table_buf[...],
                preferred_element_type=jnp.float32,
            )
            high, rest = split(mixed[:, :lanes_all] + mixed[:, lanes_all:])
            high = jnp.concatenate([high[k * edge : (k + 1) * edge] for k in range(CHUNK)], axis=1)
            rest = jnp.concatenate([rest[k * edge : (k + 1) * edge] for k in range(CHUNK)], axis=1)
            mixed = jnp.dot(
                table_y_ref[...],
                jnp.concatenate([high, high, rest], axis=0),
                preferred_element_type=jnp.float32,
            )
            for part in range(CHUNK):
                where = slice(part * lanes_all, (part + 1) * lanes_all)
                turned = pltpu.roll(mixed[edge:, where], edge, 1)
                y_buf[pl.ds(z + part, edge, stride=pitch), :] = mixed[:edge, where] + sign * turned
            return 0

        lax.fori_loop(0, edge // CHUNK, xy_step, 0, unroll=True)

        reversed_ids = jnp.where(low, (edge - lanes) % edge, edge + (lanes_all - lanes) % edge)

        def z_step(ky, total):
            mirror = lax.rem(edge - ky, edge)
            plane = y_buf[pl.ds(pl.multiple_of(ky * pitch, 8), edge), :]
            other = y_buf[pl.ds(pl.multiple_of(mirror * pitch, 8), edge), :]
            high, rest = split(jnp.concatenate([plane, other], axis=1))
            mixed = jnp.dot(
                table_y_ref[...],
                jnp.concatenate([high, high, rest], axis=0),
                preferred_element_type=jnp.float32,
            )
            front = mixed[:edge, :lanes_all] + sign * pltpu.roll(mixed[edge:, :lanes_all], edge, 1)
            back = mixed[:edge, lanes_all:] - sign * pltpu.roll(mixed[edge:, lanes_all:], edge, 1)
            back = jnp.take_along_axis(back, reversed_ids, axis=1)
            first = front * pltpu.roll(back, edge, 1)
            second = 0.5 * (front * front - back * back)
            cross = jnp.where(low, first, second) + pltpu.roll(
                jnp.where(low, second, first), edge, 1
            )
            square = cross * cross
            magnitude = jnp.sqrt(square + pltpu.roll(square, edge, 1))
            c_buf[ky] = cross
            m_buf[ky] = magnitude
            times = jnp.where((ky == 0) | (ky == half), 0.5, 1.0)
            return total + times * magnitude

        total = lax.fori_loop(
            0, half + 1, z_step, jnp.zeros((edge, lanes_all), jnp.float32), unroll=True
        )
        floor = jnp.sum(total) / float(edge**3) + 2.0 * EPSILON

        table_z = win_z_ref[slot]
        sign_w = sign[:WIN]

        def win_step(step, _):
            ratios = []
            for part in range(2):
                ky = 2 * step + part
                times = jnp.where((ky == 0) | (ky == half), 1.0, 2.0)
                ratios.append(times * c_buf[ky] / (m_buf[ky] + floor))
            high, rest = split(jnp.concatenate(ratios, axis=1))
            mixed = jnp.dot(
                table_z,
                jnp.concatenate([high, high, rest], axis=0),
                preferred_element_type=jnp.float32,
            )
            for part in range(2):
                where = slice(part * lanes_all, (part + 1) * lanes_all)
                g_buf[pl.ds(pl.multiple_of((2 * step + part) * WIN, 8), WIN), :] = mixed[
                    :WIN, where
                ] - sign_w * pltpu.roll(mixed[WIN:, where], edge, 1)
            return 0

        lax.fori_loop(0, half // 2 + 1, win_step, 0, unroll=True)

        planes = g_buf.shape[0] // WIN
        partial = jnp.concatenate(
            [g_buf[pl.ds(i, planes, stride=WIN), :] for i in range(WIN)], axis=1
        )
        mixed = jnp.dot(
            win_y_ref[slot][:, :planes],
            partial,
            precision=PRECISE,
            preferred_element_type=jnp.float32,
        )
        blocks = []
        for i in range(WIN):
            where = slice(i * lanes_all, (i + 1) * lanes_all)
            blocks.append(mixed[:WIN, where] - sign_w * pltpu.roll(mixed[WIN:, where], edge, 1))
        values = jnp.dot(
            jnp.concatenate(blocks, axis=0),
            win_x_ref[slot],
            precision=PRECISE,
            preferred_element_type=jnp.float32,
        )
        corr_ref[slot] = values

        weight = values * values
        line = lax.broadcasted_iota(jnp.int32, (WIN * WIN, lanes_all), 0)
        lane = lax.broadcasted_iota(jnp.int32, (WIN * WIN, lanes_all), 1)
        cells = float(WIN**3)
        energy = jnp.sum(weight, keepdims=True) / cells
        places = (line // WIN, line % WIN, lane)
        shifts = [
            (jnp.sum(weight * place.astype(jnp.float32), keepdims=True) / cells
             + energy * fields_ref[5 + axis, slot].astype(jnp.float32))
            / (energy + EPSILON)
            for axis, place in enumerate(places)
        ]
        views = sums_ref.shape[0]
        view = lax.broadcasted_iota(jnp.int32, (views, lanes_all), 0)
        entry = lax.broadcasted_iota(jnp.int32, (views, lanes_all), 1)
        center_z = (own_index.astype(jnp.float32) * edge + 0.5 * edge) / (edge * slab_count)
        center_x = (start_a.astype(jnp.float32) + 0.5 * edge) / (2.0 * edge)

        def center(index):
            return jnp.where(
                index == 0,
                center_z,
                jnp.where(index == 1, 0.5, jnp.where(index == 2, center_x, 1.0)),
            )

        hit_a = (view == fields_ref[0, slot]).astype(jnp.float32)
        hit_b = (view == fields_ref[2, slot]).astype(jnp.float32)
        normal = (hit_a + hit_b) * center(entry // 4) * center(entry % 4)
        after = jnp.maximum(entry - 16, 0)
        which = after % 3
        shift = jnp.where(which == 0, shifts[0], jnp.where(which == 1, shifts[1], shifts[2]))
        rhs = (hit_a - hit_b) * center(after // 3) * shift
        sums_ref[...] += jnp.where(entry < 16, normal, jnp.where(entry < 28, rhs, 0.0)) * (
            energy / pair_total
        )
        spot = lax.broadcasted_iota(jnp.int32, shift_ref.shape, 0)
        column = lax.broadcasted_iota(jnp.int32, shift_ref.shape, 1)
        for axis in range(3):
            shift_ref[...] += jnp.where((spot == axis) & (column == slot), shifts[axis], 0.0)
        return 0

    lax.fori_loop(0, count, pair_step, 0)


def pairs(volumes, from_above, from_below, pair_fields, pair_counts, tables, slab_count):
    view_count, edge = volumes.shape[0], volumes.shape[1]
    cap = pair_fields.shape[1]
    lanes = 2 * edge
    half = edge // 2
    table_x, table_y = static_tables(edge)
    smem = pl.BlockSpec(memory_space=pltpu.SMEM)
    vmem = pl.BlockSpec(memory_space=pltpu.VMEM)
    anywhere = pl.BlockSpec(memory_space=pltpu.HBM)

    def kernel(*refs):
        pair_kernel(slab_count, float(cap * slab_count), *refs)

    return pl.pallas_call(
        kernel,
        out_shape=(
            jax.ShapeDtypeStruct((cap, WIN * WIN, lanes), jnp.float32),
            jax.ShapeDtypeStruct((8, lanes), jnp.float32),
            jax.ShapeDtypeStruct((view_count, lanes), jnp.float32),
        ),
        in_specs=[smem, smem, anywhere, anywhere, anywhere] + [vmem] * 5,
        out_specs=(vmem, vmem, vmem),
        scratch_shapes=[
            pltpu.VMEM((2, edge, edge, lanes), volumes.dtype),
            pltpu.VMEM((2, edge, edge, lanes), volumes.dtype),
            pltpu.SemaphoreType.DMA((2, 2)),
            pltpu.VMEM((2 * lanes, 2 * lanes), jnp.bfloat16),
            pltpu.VMEM((edge * (edge + GAP), lanes), jnp.float32),
            pltpu.VMEM((half + 2, edge, lanes), jnp.float32),
            pltpu.VMEM((half + 2, edge, lanes), jnp.float32),
            pltpu.VMEM(((half + 2) * WIN, lanes), jnp.float32),
        ],
        compiler_params=pltpu.CompilerParams(vmem_limit_bytes=40 * 2**20),
        name="pairs",
    )(
        pair_fields,
        pair_counts,
        volumes,
        from_above,
        from_below,
        jnp.asarray(table_x),
        jnp.asarray(table_y),
        *tables,
    )


def sum_kernel(part_ref, out_ref, held, send_sems, recv_sems):
    count = lax.axis_size("slab")
    own = lax.axis_index("slab")
    barrier = pltpu.get_barrier_semaphore()
    for step in range(1, count):
        peer = lax.rem(own + step, count)
        pl.semaphore_signal(
            barrier, inc=1, device_id={"slab": peer}, device_id_type=pl.DeviceIdType.MESH
        )
    pl.semaphore_wait(barrier, count - 1)

    def copy_to(peer, source):
        return pltpu.make_async_remote_copy(
            src_ref=part_ref,
            dst_ref=held.at[source],
            send_sem=send_sems.at[peer],
            recv_sem=recv_sems.at[source],
            device_id={"slab": peer},
            device_id_type=pl.DeviceIdType.MESH,
        )

    for step in range(1, count):
        copy_to(lax.rem(own + step, count), own).start()
    held[own] = part_ref[...]
    for step in range(1, count):
        peer = lax.rem(own + step, count)
        copy_to(peer, own).wait_send()
        copy_to(peer, peer).wait_recv()
    total = held[0]
    for index in range(1, count):
        total = total + held[index]
    out_ref[...] = total


def summed(part):
    count = lax.axis_size("slab")
    return pl.pallas_call(
        sum_kernel,
        out_shape=jax.ShapeDtypeStruct(part.shape, part.dtype),
        in_specs=[pl.BlockSpec(memory_space=pltpu.VMEM)],
        out_specs=pl.BlockSpec(memory_space=pltpu.VMEM),
        scratch_shapes=[
            pltpu.VMEM((count,) + part.shape, part.dtype),
            pltpu.SemaphoreType.DMA((count,)),
            pltpu.SemaphoreType.DMA((count,)),
        ],
        compiler_params=pltpu.CompilerParams(collective_id=0, has_side_effects=True),
        name="slab_sum",
    )(part)


def on_device(volumes, pair_fields, pair_counts):
    cap = pair_fields.shape[1]
    edge = volumes.shape[1]
    slab_count = lax.axis_size("slab")
    live = jnp.arange(cap, dtype=jnp.int32) < pair_counts[0]
    listed = jnp.where(live[None, :], pair_fields, 0)
    listed = jnp.pad(listed, ((0, 0), (0, 2 * edge - cap)))
    tables = window_tables(pair_fields, edge)
    from_above, from_below = exchanged(volumes, listed, cap)
    corr, shifts, sums = pairs(
        volumes, from_above, from_below, pair_fields, pair_counts, tables, slab_count
    )
    sums = summed(sums)
    return (
        corr[:, :, :WIN].reshape(cap, WIN**3),
        shifts[:3, :cap],
        sums[:, :16].reshape(-1, 4, 4),
        sums[:, 16:28].reshape(-1, 4, 3),
    )


def solution(mesh):
    in_specs = (P("tm", "slab", None, None), P(None, ("tm", "slab")), P(("tm", "slab")))
    out_specs = (
        P(("tm", "slab"), None),
        P(None, ("tm", "slab")),
        P("tm", None, None),
        P("tm", None, None),
    )
    return jax.shard_map(
        on_device, mesh=mesh, in_specs=in_specs, out_specs=out_specs, check_vma=False
    )
```

```python
import functools
import math

import jax
import jax.numpy as jnp
import numpy as np
from jax import lax
from jax.experimental import pallas as pl
from jax.experimental.pallas import tpu as pltpu
from jax.sharding import PartitionSpec as P

WIN = 8
NBR = 2
EPSILON = 1e-06
GAP = 8
PIECES = 4
CHUNK = 16
PRECISE = lax.Precision.HIGHEST


def split(values):
    high = values.astype(jnp.bfloat16)
    return high, (values - high.astype(jnp.float32)).astype(jnp.bfloat16)


def split_outside(values):
    high = lax.reduce_precision(values, 8, 7)
    return high.astype(jnp.bfloat16), (values - high).astype(jnp.bfloat16)


def static_tables(edge):
    ids = np.arange(edge)
    cells = np.arange(2 * edge) % edge
    angles = 2 * np.pi * (np.outer(cells, ids) % edge) / edge
    table_a = np.concatenate([np.cos(angles), -np.sin(angles)], axis=1)
    table_b = np.concatenate([np.sin(angles), np.cos(angles)], axis=1)
    table_x = np.concatenate([table_a, table_b], axis=0).astype(np.float32)
    high = table_x.astype(jnp.bfloat16)
    low = (table_x - high.astype(np.float32)).astype(jnp.bfloat16)
    table_x = np.concatenate([high, low], axis=1).astype(np.float32)
    angles = 2 * np.pi * (np.outer(ids, ids) % edge) / edge
    table_y = np.concatenate([np.cos(angles), np.sin(angles)], axis=0).astype(np.float32)
    high = table_y.astype(jnp.bfloat16)
    low = (table_y - high.astype(np.float32)).astype(jnp.bfloat16)
    return table_x, np.concatenate([high, low, high], axis=1)


def window_tables(fields, edge):
    steps = jnp.arange(WIN, dtype=jnp.int32)
    ids = jnp.arange(edge, dtype=jnp.int32)
    offsets = fields[5:8] + jnp.stack([0 * fields[1], 0 * fields[1], fields[1] - fields[4]])
    product = jnp.mod((offsets[:, :, None] + steps)[..., None] * ids, edge)
    angles = (2.0 * math.pi / edge) * product.astype(jnp.float32)
    cos_all, sin_all = jnp.cos(angles), jnp.sin(angles)
    both = jnp.concatenate([cos_all, sin_all], axis=2)
    high, low = split_outside(both[0])
    table_z = jnp.concatenate([high, low, high], axis=2)
    table_y = jnp.pad(both[1], ((0, 0), (0, 0), (0, edge)))
    table_x = jnp.concatenate([cos_all[2], -sin_all[2]], axis=2) / edge**1.5
    table_x = jnp.pad(table_x, ((0, 0), (0, 2 * edge - WIN), (0, 0)))
    return table_z, table_y, jnp.swapaxes(table_x, 1, 2)


def find_request(fields, slots, direction, level):
    seen = jnp.int32(0)
    view, anchor = jnp.int32(0), jnp.int32(0)
    for slot in range(slots):
        wanted = fields[3, slot] == direction
        take = wanted & (seen == level)
        view = jnp.where(take, fields[2, slot], view)
        anchor = jnp.where(take, fields[4, slot], anchor)
        seen = seen + wanted.astype(jnp.int32)
    return view, anchor


def exchange_kernel(
    slots,
    list_ref,
    volumes_ref,
    above_ref,
    below_ref,
    held,
    list_in,
    list_smem,
    packed,
    local_sems,
    list_send,
    list_recv,
    send_sems,
    recv_sems,
):
    edge = above_ref.shape[0]
    cells = edge // PIECES
    count = lax.axis_size("slab")
    own = lax.axis_index("slab")
    load = pltpu.make_async_copy(volumes_ref, held, local_sems.at[0])
    load.start()
    list_in[...] = jnp.zeros_like(list_in)
    present = (own > 0, own < count - 1)
    peers = (lax.rem(own + count - 1, count), lax.rem(own + 1, count))
    results = (above_ref, below_ref)
    barrier = pltpu.get_barrier_semaphore()

    def on(side, action):
        pl.when(present[side])(action)

    for side in range(2):
        on(
            side,
            lambda side=side: pl.semaphore_signal(
                barrier,
                inc=1,
                device_id={"slab": peers[side]},
                device_id_type=pl.DeviceIdType.MESH,
            ),
        )
    pl.semaphore_wait(barrier, present[0].astype(jnp.int32) + present[1].astype(jnp.int32))

    def list_copy(side):
        return pltpu.make_async_remote_copy(
            src_ref=list_ref,
            dst_ref=list_in.at[1 - side],
            send_sem=list_send.at[side],
            recv_sem=list_recv.at[1 - side],
            device_id={"slab": peers[side]},
            device_id_type=pl.DeviceIdType.MESH,
        )

    def list_arrival(side):
        return pltpu.make_async_remote_copy(
            src_ref=list_ref,
            dst_ref=list_in.at[side],
            send_sem=list_send.at[side],
            recv_sem=list_recv.at[side],
            device_id={"slab": peers[side]},
            device_id_type=pl.DeviceIdType.MESH,
        )

    for side in range(2):
        on(side, lambda side=side: list_copy(side).start())
    for side in range(2):
        on(side, lambda side=side: list_arrival(side).wait_recv())
    to_smem = pltpu.make_async_copy(list_in, list_smem, local_sems.at[1])
    to_smem.start()
    to_smem.wait()
    picks = []
    for side, direction in enumerate((1, -1)):
        picks.append(
            [find_request(list_smem.at[side], slots, direction, level) for level in range(NBR)]
        )
    load.wait()

    def pack_piece(side, piece):
        (first_view, first_x), (second_view, second_x) = picks[side]

        def step(index, _):
            z = piece * cells + index
            lanes = lax.broadcasted_iota(jnp.int32, (edge, 2 * edge), 1)
            first = held[first_view, z].astype(jnp.float32)
            second = held[second_view, z].astype(jnp.float32)
            straight = jnp.where(lanes < edge, first, second)
            turned = pltpu.roll(jnp.where(lanes < edge, second, first), edge, 1)
            keep = ((lanes < edge) & (lanes >= first_x)) | (
                (lanes >= edge) & (lanes < edge + second_x)
            )
            packed[side, z] = jnp.where(keep, straight, turned).astype(jnp.bfloat16)
            return 0

        lax.fori_loop(0, cells, step, 0, unroll=8)

    def window_copy(side, piece):
        where = pl.ds(piece * cells, cells)
        return pltpu.make_async_remote_copy(
            src_ref=packed.at[side, where],
            dst_ref=results[side].at[where],
            send_sem=send_sems.at[side, piece],
            recv_sem=recv_sems.at[side, piece],
            device_id={"slab": peers[side]},
            device_id_type=pl.DeviceIdType.MESH,
        )

    def window_arrival(side, piece):
        where = pl.ds(piece * cells, cells)
        return pltpu.make_async_remote_copy(
            src_ref=packed.at[side, where],
            dst_ref=results[1 - side].at[where],
            send_sem=send_sems.at[side, piece],
            recv_sem=recv_sems.at[1 - side, piece],
            device_id={"slab": peers[side]},
            device_id_type=pl.DeviceIdType.MESH,
        )

    items = [(side, piece) for piece in range(PIECES) for side in range(2)]
    for number, (side, piece) in enumerate(items):
        pack_piece(side, piece)
        if number:
            previous = items[number - 1]
            on(previous[0], lambda previous=previous: window_copy(*previous).start())
    on(items[-1][0], lambda: window_copy(*items[-1]).start())
    for item in items:
        on(item[0], lambda item=item: window_arrival(*item).wait_recv())
    for item in items:
        on(item[0], lambda item=item: window_copy(*item).wait_send())
    for side in range(2):
        on(side, lambda side=side: list_copy(side).wait_send())


def exchanged(volumes, listed, slots):
    edge = volumes.shape[1]
    shape = jax.ShapeDtypeStruct(volumes.shape[1:], volumes.dtype)
    vmem = pl.BlockSpec(memory_space=pltpu.VMEM)
    return pl.pallas_call(
        functools.partial(exchange_kernel, slots),
        out_shape=(shape, shape),
        in_specs=[vmem, pl.BlockSpec(memory_space=pltpu.HBM)],
        out_specs=(vmem, vmem),
        scratch_shapes=[
            pltpu.VMEM(volumes.shape, volumes.dtype),
            pltpu.VMEM((2,) + listed.shape, listed.dtype),
            pltpu.SMEM((2,) + listed.shape, listed.dtype),
            pltpu.VMEM((2,) + volumes.shape[1:], volumes.dtype),
            pltpu.SemaphoreType.DMA((2,)),
            pltpu.SemaphoreType.DMA((2,)),
            pltpu.SemaphoreType.DMA((2,)),
            pltpu.SemaphoreType.DMA((2, PIECES)),
            pltpu.SemaphoreType.DMA((2, PIECES)),
        ],
        compiler_params=pltpu.CompilerParams(collective_id=1, has_side_effects=True),
        name="exchange",
    )(listed, volumes)


def pair_kernel(
    slab_count,
    pair_total,
    fields_ref,
    counts_ref,
    volumes_ref,
    above_ref,
    below_ref,
    table_x_ref,
    table_y_ref,
    win_z_ref,
    win_y_ref,
    win_x_ref,
    corr_ref,
    shift_ref,
    sums_ref,
    a_buf,
    b_buf,
    sems,
    table_buf,
    y_buf,
    c_buf,
    m_buf,
    g_buf,
):
    edge = volumes_ref.shape[1]
    lanes_all = 2 * edge
    half = edge // 2
    cap = fields_ref.shape[1]
    pitch = edge + GAP
    count = counts_ref[0]
    own_index = lax.axis_index("slab")

    def fetch(slot, start):
        buf = lax.rem(slot, 2)
        copy_a = pltpu.make_async_copy(
            volumes_ref.at[fields_ref[0, slot]], a_buf.at[buf], sems.at[0, buf]
        )
        copy_b = pltpu.make_async_copy(
            volumes_ref.at[fields_ref[2, slot]], b_buf.at[buf], sems.at[1, buf]
        )
        if not start:
            copy_a.wait()
            copy_b.wait()
            return
        copy_a.start()
        direction = fields_ref[3, slot]

        @pl.when(direction == 0)
        def _():
            copy_b.start()

        @pl.when(direction == 1)
        def _():
            pltpu.make_async_copy(above_ref, b_buf.at[buf], sems.at[1, buf]).start()

        @pl.when(direction == -1)
        def _():
            pltpu.make_async_copy(below_ref, b_buf.at[buf], sems.at[1, buf]).start()

    fetch(jnp.int32(0), True)
    corr_ref[...] = jnp.zeros_like(corr_ref)
    shift_ref[...] = jnp.zeros_like(shift_ref)
    sums_ref[...] = jnp.zeros_like(sums_ref)
    c_buf[half + 1] = jnp.zeros((edge, lanes_all), jnp.float32)
    m_buf[half + 1] = jnp.zeros((edge, lanes_all), jnp.float32)

    def pair_step(slot, _):
        buf = lax.rem(slot, 2)

        @pl.when(slot + 1 < count)
        def _():
            fetch(slot + 1, True)

        direction = fields_ref[3, slot]
        rank = jnp.int32(0)
        for other in range(cap):
            rank = rank + ((fields_ref[3, other] == direction) & (other < slot)).astype(jnp.int32)
        start_a = fields_ref[1, slot]
        start_b = jnp.where(direction == 0, fields_ref[4, slot], edge * rank)
        rows = lax.broadcasted_iota(jnp.int32, (lanes_all, 2 * lanes_all), 0)
        for part, start in enumerate((start_a, start_b)):
            where = pl.ds(part * lanes_all, lanes_all)
            inside = (rows >= start) & (rows < start + edge)
            table_buf[where, :] = jnp.where(inside, table_x_ref[where, :], 0.0).astype(jnp.bfloat16)
        fetch(slot, False)

        lanes = lax.broadcasted_iota(jnp.int32, (edge, lanes_all), 1)
        low = lanes < edge
        sign = jnp.where(low, 1.0, -1.0)

        def xy_step(step, _):
            z = CHUNK * step
            left = a_buf[buf, pl.ds(z, CHUNK)].reshape(CHUNK * edge, lanes_all)
            right = b_buf[buf, pl.ds(z, CHUNK)].reshape(CHUNK * edge, lanes_all)
            mixed = jnp.dot(
                jnp.concatenate([left, right], axis=1),
                table_buf[...],
                preferred_element_type=jnp.float32,
            )
            high, rest = split(mixed[:, :lanes_all] + mixed[:, lanes_all:])
            high = jnp.concatenate([high[k * edge : (k + 1) * edge] for k in range(CHUNK)], axis=1)
            rest = jnp.concatenate([rest[k * edge : (k + 1) * edge] for k in range(CHUNK)], axis=1)
            mixed = jnp.dot(
                table_y_ref[...],
                jnp.concatenate([high, high, rest], axis=0),
                preferred_element_type=jnp.float32,
            )
            for part in range(CHUNK):
                where = slice(part * lanes_all, (part + 1) * lanes_all)
                turned = pltpu.roll(mixed[edge:, where], edge, 1)
                y_buf[pl.ds(z + part, edge, stride=pitch), :] = mixed[:edge, where] + sign * turned
            return 0

        lax.fori_loop(0, edge // CHUNK, xy_step, 0, unroll=True)

        reversed_ids = jnp.where(low, (edge - lanes) % edge, edge + (lanes_all - lanes) % edge)

        def z_step(ky, total):
            mirror = lax.rem(edge - ky, edge)
            plane = y_buf[pl.ds(pl.multiple_of(ky * pitch, 8), edge), :]
            other = y_buf[pl.ds(pl.multiple_of(mirror * pitch, 8), edge), :]
            high, rest = split(jnp.concatenate([plane, other], axis=1))
            mixed = jnp.dot(
                table_y_ref[...],
                jnp.concatenate([high, high, rest], axis=0),
                preferred_element_type=jnp.float32,
            )
            front = mixed[:edge, :lanes_all] + sign * pltpu.roll(mixed[edge:, :lanes_all], edge, 1)
            back = mixed[:edge, lanes_all:] - sign * pltpu.roll(mixed[edge:, lanes_all:], edge, 1)
            back = jnp.take_along_axis(back, reversed_ids, axis=1)
            first = front * pltpu.roll(back, edge, 1)
            second = 0.5 * (front * front - back * back)
            cross = jnp.where(low, first, second) + pltpu.roll(
                jnp.where(low, second, first), edge, 1
            )
            square = cross * cross
            magnitude = jnp.sqrt(square + pltpu.roll(square, edge, 1))
            c_buf[ky] = cross
            m_buf[ky] = magnitude
            times = jnp.where((ky == 0) | (ky == half), 0.5, 1.0)
            return total + times * magnitude

        total = lax.fori_loop(
            0, half + 1, z_step, jnp.zeros((edge, lanes_all), jnp.float32), unroll=True
        )
        floor = jnp.sum(total) / float(edge**3) + 2.0 * EPSILON

        table_z = win_z_ref[slot]
        sign_w = sign[:WIN]

        def win_step(step, _):
            ratios = []
            for part in range(2):
                ky = 2 * step + part
                times = jnp.where((ky == 0) | (ky == half), 1.0, 2.0)
                ratios.append(times * c_buf[ky] / (m_buf[ky] + floor))
            high, rest = split(jnp.concatenate(ratios, axis=1))
            mixed = jnp.dot(
                table_z,
                jnp.concatenate([high, high, rest], axis=0),
                preferred_element_type=jnp.float32,
            )
            for part in range(2):
                where = slice(part * lanes_all, (part + 1) * lanes_all)
                g_buf[pl.ds(pl.multiple_of((2 * step + part) * WIN, 8), WIN), :] = mixed[
                    :WIN, where
                ] - sign_w * pltpu.roll(mixed[WIN:, where], edge, 1)
            return 0

        lax.fori_loop(0, half // 2 + 1, win_step, 0, unroll=True)

        planes = g_buf.shape[0] // WIN
        partial = jnp.concatenate(
            [g_buf[pl.ds(i, planes, stride=WIN), :] for i in range(WIN)], axis=1
        )
        mixed = jnp.dot(
            win_y_ref[slot][:, :planes],
            partial,
            precision=PRECISE,
            preferred_element_type=jnp.float32,
        )
        blocks = []
        for i in range(WIN):
            where = slice(i * lanes_all, (i + 1) * lanes_all)
            blocks.append(mixed[:WIN, where] - sign_w * pltpu.roll(mixed[WIN:, where], edge, 1))
        values = jnp.dot(
            jnp.concatenate(blocks, axis=0),
            win_x_ref[slot],
            precision=PRECISE,
            preferred_element_type=jnp.float32,
        )
        corr_ref[slot] = values

        weight = values * values
        line = lax.broadcasted_iota(jnp.int32, (WIN * WIN, lanes_all), 0)
        lane = lax.broadcasted_iota(jnp.int32, (WIN * WIN, lanes_all), 1)
        cells = float(WIN**3)
        energy = jnp.sum(weight, keepdims=True) / cells
        places = (line // WIN, line % WIN, lane)
        shifts = [
            (jnp.sum(weight * place.astype(jnp.float32), keepdims=True) / cells
             + energy * fields_ref[5 + axis, slot].astype(jnp.float32))
            / (energy + EPSILON)
            for axis, place in enumerate(places)
        ]
        views = sums_ref.shape[0]
        view = lax.broadcasted_iota(jnp.int32, (views, lanes_all), 0)
        entry = lax.broadcasted_iota(jnp.int32, (views, lanes_all), 1)
        center_z = (own_index.astype(jnp.float32) * edge + 0.5 * edge) / (edge * slab_count)
        center_x = (start_a.astype(jnp.float32) + 0.5 * edge) / (2.0 * edge)

        def center(index):
            return jnp.where(
                index == 0,
                center_z,
                jnp.where(index == 1, 0.5, jnp.where(index == 2, center_x, 1.0)),
            )

        hit_a = (view == fields_ref[0, slot]).astype(jnp.float32)
        hit_b = (view == fields_ref[2, slot]).astype(jnp.float32)
        normal = (hit_a + hit_b) * center(entry // 4) * center(entry % 4)
        after = jnp.maximum(entry - 16, 0)
        which = after % 3
        shift = jnp.where(which == 0, shifts[0], jnp.where(which == 1, shifts[1], shifts[2]))
        rhs = (hit_a - hit_b) * center(after // 3) * shift
        sums_ref[...] += jnp.where(entry < 16, normal, jnp.where(entry < 28, rhs, 0.0)) * (
            energy / pair_total
        )
        spot = lax.broadcasted_iota(jnp.int32, shift_ref.shape, 0)
        column = lax.broadcasted_iota(jnp.int32, shift_ref.shape, 1)
        for axis in range(3):
            shift_ref[...] += jnp.where((spot == axis) & (column == slot), shifts[axis], 0.0)
        return 0

    lax.fori_loop(0, count, pair_step, 0)


def pairs(volumes, from_above, from_below, pair_fields, pair_counts, tables, slab_count):
    view_count, edge = volumes.shape[0], volumes.shape[1]
    cap = pair_fields.shape[1]
    lanes = 2 * edge
    half = edge // 2
    table_x, table_y = static_tables(edge)
    smem = pl.BlockSpec(memory_space=pltpu.SMEM)
    vmem = pl.BlockSpec(memory_space=pltpu.VMEM)
    anywhere = pl.BlockSpec(memory_space=pltpu.HBM)

    def kernel(*refs):
        pair_kernel(slab_count, float(cap * slab_count), *refs)

    return pl.pallas_call(
        kernel,
        out_shape=(
            jax.ShapeDtypeStruct((cap, WIN * WIN, lanes), jnp.float32),
            jax.ShapeDtypeStruct((8, lanes), jnp.float32),
            jax.ShapeDtypeStruct((view_count, lanes), jnp.float32),
        ),
        in_specs=[smem, smem, anywhere, anywhere, anywhere] + [vmem] * 5,
        out_specs=(vmem, vmem, vmem),
        scratch_shapes=[
            pltpu.VMEM((2, edge, edge, lanes), volumes.dtype),
            pltpu.VMEM((2, edge, edge, lanes), volumes.dtype),
            pltpu.SemaphoreType.DMA((2, 2)),
            pltpu.VMEM((2 * lanes, 2 * lanes), jnp.bfloat16),
            pltpu.VMEM((edge * (edge + GAP), lanes), jnp.float32),
            pltpu.VMEM((half + 2, edge, lanes), jnp.float32),
            pltpu.VMEM((half + 2, edge, lanes), jnp.float32),
            pltpu.VMEM(((half + 2) * WIN, lanes), jnp.float32),
        ],
        name="pairs",
    )(
        pair_fields,
        pair_counts,
        volumes,
        from_above,
        from_below,
        jnp.asarray(table_x),
        jnp.asarray(table_y),
        *tables,
    )


def sum_kernel(part_ref, out_ref, held, send_sems, recv_sems):
    count = lax.axis_size("slab")
    own = lax.axis_index("slab")
    barrier = pltpu.get_barrier_semaphore()
    for step in range(1, count):
        peer = lax.rem(own + step, count)
        pl.semaphore_signal(
            barrier, inc=1, device_id={"slab": peer}, device_id_type=pl.DeviceIdType.MESH
        )
    pl.semaphore_wait(barrier, count - 1)

    def copy_to(peer, source):
        return pltpu.make_async_remote_copy(
            src_ref=part_ref,
            dst_ref=held.at[source],
            send_sem=send_sems.at[peer],
            recv_sem=recv_sems.at[source],
            device_id={"slab": peer},
            device_id_type=pl.DeviceIdType.MESH,
        )

    for step in range(1, count):
        copy_to(lax.rem(own + step, count), own).start()
    held[own] = part_ref[...]
    for step in range(1, count):
        peer = lax.rem(own + step, count)
        copy_to(peer, own).wait_send()
        copy_to(peer, peer).wait_recv()
    total = held[0]
    for index in range(1, count):
        total = total + held[index]
    out_ref[...] = total


def summed(part):
    count = lax.axis_size("slab")
    return pl.pallas_call(
        sum_kernel,
        out_shape=jax.ShapeDtypeStruct(part.shape, part.dtype),
        in_specs=[pl.BlockSpec(memory_space=pltpu.VMEM)],
        out_specs=pl.BlockSpec(memory_space=pltpu.VMEM),
        scratch_shapes=[
            pltpu.VMEM((count,) + part.shape, part.dtype),
            pltpu.SemaphoreType.DMA((count,)),
            pltpu.SemaphoreType.DMA((count,)),
        ],
        compiler_params=pltpu.CompilerParams(collective_id=0, has_side_effects=True),
        name="slab_sum",
    )(part)


def on_device(volumes, pair_fields, pair_counts):
    cap = pair_fields.shape[1]
    edge = volumes.shape[1]
    slab_count = lax.axis_size("slab")
    live = jnp.arange(cap, dtype=jnp.int32) < pair_counts[0]
    listed = jnp.where(live[None, :], pair_fields, 0)
    listed = jnp.pad(listed, ((0, 0), (0, 2 * edge - cap)))
    tables = window_tables(pair_fields, edge)
    from_above, from_below = exchanged(volumes, listed, cap)
    corr, shifts, sums = pairs(
        volumes, from_above, from_below, pair_fields, pair_counts, tables, slab_count
    )
    sums = summed(sums)
    return (
        corr[:, :, :WIN].reshape(cap, WIN**3),
        shifts[:3, :cap],
        sums[:, :16].reshape(-1, 4, 4),
        sums[:, 16:28].reshape(-1, 4, 3),
    )


def solution(mesh):
    in_specs = (P("tm", "slab", None, None), P(None, ("tm", "slab")), P(("tm", "slab")))
    out_specs = (
        P(("tm", "slab"), None),
        P(None, ("tm", "slab")),
        P("tm", None, None),
        P("tm", None, None),
    )
    return jax.shard_map(
        on_device, mesh=mesh, in_specs=in_specs, out_specs=out_specs, check_vma=False
    )
```

```python
import functools
import math

import jax
import jax.numpy as jnp
import numpy as np
from jax import lax
from jax.experimental import pallas as pl
from jax.experimental.pallas import tpu as pltpu
from jax.sharding import PartitionSpec as P

WIN = 8
NBR = 2
EPSILON = 1e-06
GAP = 8
PIECES = 4
CHUNK = 16
PRECISE = lax.Precision.HIGHEST


def split(values):
    high = values.astype(jnp.bfloat16)
    return high, (values - high.astype(jnp.float32)).astype(jnp.bfloat16)


def split_outside(values):
    high = lax.reduce_precision(values, 8, 7)
    return high.astype(jnp.bfloat16), (values - high).astype(jnp.bfloat16)


def static_tables(edge):
    ids = np.arange(edge)
    cells = np.arange(2 * edge) % edge
    angles = 2 * np.pi * (np.outer(cells, ids) % edge) / edge
    table_a = np.concatenate([np.cos(angles), -np.sin(angles)], axis=1)
    table_b = np.concatenate([np.sin(angles), np.cos(angles)], axis=1)
    table_x = np.concatenate([table_a, table_b], axis=0).astype(np.float32)
    high = table_x.astype(jnp.bfloat16)
    low = (table_x - high.astype(np.float32)).astype(jnp.bfloat16)
    table_x = np.concatenate([high, low], axis=1).astype(np.float32)
    angles = 2 * np.pi * (np.outer(ids, ids) % edge) / edge
    table_y = np.concatenate([np.cos(angles), np.sin(angles)], axis=0).astype(np.float32)
    high = table_y.astype(jnp.bfloat16)
    low = (table_y - high.astype(np.float32)).astype(jnp.bfloat16)
    return table_x, np.concatenate([high, low, high], axis=1)


def window_tables(fields, edge):
    steps = jnp.arange(WIN, dtype=jnp.int32)
    ids = jnp.arange(edge, dtype=jnp.int32)
    offsets = fields[5:8] + jnp.stack([0 * fields[1], 0 * fields[1], fields[1] - fields[4]])
    product = jnp.mod((offsets[:, :, None] + steps)[..., None] * ids, edge)
    angles = (2.0 * math.pi / edge) * product.astype(jnp.float32)
    cos_all, sin_all = jnp.cos(angles), jnp.sin(angles)
    both = jnp.concatenate([cos_all, sin_all], axis=2)
    high, low = split_outside(both[0])
    table_z = jnp.concatenate([high, low, high], axis=2)
    table_y = jnp.pad(both[1], ((0, 0), (0, 0), (0, edge)))
    table_x = jnp.concatenate([cos_all[2], -sin_all[2]], axis=2) / edge**1.5
    table_x = jnp.pad(table_x, ((0, 0), (0, 2 * edge - WIN), (0, 0)))
    return table_z, table_y, jnp.swapaxes(table_x, 1, 2)


def find_request(fields, slots, direction, level):
    seen = jnp.int32(0)
    view, anchor = jnp.int32(0), jnp.int32(0)
    for slot in range(slots):
        wanted = fields[3, slot] == direction
        take = wanted & (seen == level)
        view = jnp.where(take, fields[2, slot], view)
        anchor = jnp.where(take, fields[4, slot], anchor)
        seen = seen + wanted.astype(jnp.int32)
    return view, anchor


def exchange_kernel(
    slots,
    list_ref,
    volumes_ref,
    above_ref,
    below_ref,
    held,
    list_in,
    list_smem,
    packed,
    local_sems,
    list_send,
    list_recv,
    send_sems,
    recv_sems,
):
    edge = above_ref.shape[0]
    cells = edge // PIECES
    count = lax.axis_size("slab")
    own = lax.axis_index("slab")
    load = pltpu.make_async_copy(volumes_ref, held, local_sems.at[0])
    load.start()
    list_in[...] = jnp.zeros_like(list_in)
    present = (own > 0, own < count - 1)
    peers = (lax.rem(own + count - 1, count), lax.rem(own + 1, count))
    results = (above_ref, below_ref)
    barrier = pltpu.get_barrier_semaphore()

    def on(side, action):
        pl.when(present[side])(action)

    for side in range(2):
        on(
            side,
            lambda side=side: pl.semaphore_signal(
                barrier,
                inc=1,
                device_id={"slab": peers[side]},
                device_id_type=pl.DeviceIdType.MESH,
            ),
        )
    pl.semaphore_wait(barrier, present[0].astype(jnp.int32) + present[1].astype(jnp.int32))

    def list_copy(side):
        return pltpu.make_async_remote_copy(
            src_ref=list_ref,
            dst_ref=list_in.at[1 - side],
            send_sem=list_send.at[side],
            recv_sem=list_recv.at[1 - side],
            device_id={"slab": peers[side]},
            device_id_type=pl.DeviceIdType.MESH,
        )

    def list_arrival(side):
        return pltpu.make_async_remote_copy(
            src_ref=list_ref,
            dst_ref=list_in.at[side],
            send_sem=list_send.at[side],
            recv_sem=list_recv.at[side],
            device_id={"slab": peers[side]},
            device_id_type=pl.DeviceIdType.MESH,
        )

    for side in range(2):
        on(side, lambda side=side: list_copy(side).start())
    for side in range(2):
        on(side, lambda side=side: list_arrival(side).wait_recv())
    to_smem = pltpu.make_async_copy(list_in, list_smem, local_sems.at[1])
    to_smem.start()
    to_smem.wait()
    picks = []
    for side, direction in enumerate((1, -1)):
        picks.append(
            [find_request(list_smem.at[side], slots, direction, level) for level in range(NBR)]
        )
    load.wait()

    def pack_piece(side, piece):
        (first_view, first_x), (second_view, second_x) = picks[side]

        def step(index, _):
            z = piece * cells + index
            lanes = lax.broadcasted_iota(jnp.int32, (edge, 2 * edge), 1)
            first = held[first_view, z].astype(jnp.float32)
            second = held[second_view, z].astype(jnp.float32)
            straight = jnp.where(lanes < edge, first, second)
            turned = pltpu.roll(jnp.where(lanes < edge, second, first), edge, 1)
            keep = ((lanes < edge) & (lanes >= first_x)) | (
                (lanes >= edge) & (lanes < edge + second_x)
            )
            packed[side, z] = jnp.where(keep, straight, turned).astype(jnp.bfloat16)
            return 0

        lax.fori_loop(0, cells, step, 0, unroll=8)

    def window_copy(side, piece):
        where = pl.ds(piece * cells, cells)
        return pltpu.make_async_remote_copy(
            src_ref=packed.at[side, where],
            dst_ref=results[side].at[where],
            send_sem=send_sems.at[side, piece],
            recv_sem=recv_sems.at[side, piece],
            device_id={"slab": peers[side]},
            device_id_type=pl.DeviceIdType.MESH,
        )

    def window_arrival(side, piece):
        where = pl.ds(piece * cells, cells)
        return pltpu.make_async_remote_copy(
            src_ref=packed.at[side, where],
            dst_ref=results[1 - side].at[where],
            send_sem=send_sems.at[side, piece],
            recv_sem=recv_sems.at[1 - side, piece],
            device_id={"slab": peers[side]},
            device_id_type=pl.DeviceIdType.MESH,
        )

    items = [(side, piece) for piece in range(PIECES) for side in range(2)]
    for number, (side, piece) in enumerate(items):
        pack_piece(side, piece)
        if number:
            previous = items[number - 1]
            on(previous[0], lambda previous=previous: window_copy(*previous).start())
    on(items[-1][0], lambda: window_copy(*items[-1]).start())
    for item in items:
        on(item[0], lambda item=item: window_arrival(*item).wait_recv())
    for item in items:
        on(item[0], lambda item=item: window_copy(*item).wait_send())
    for side in range(2):
        on(side, lambda side=side: list_copy(side).wait_send())


def exchanged(volumes, listed, slots):
    edge = volumes.shape[1]
    shape = jax.ShapeDtypeStruct(volumes.shape[1:], volumes.dtype)
    vmem = pl.BlockSpec(memory_space=pltpu.VMEM)
    return pl.pallas_call(
        functools.partial(exchange_kernel, slots),
        out_shape=(shape, shape),
        in_specs=[vmem, pl.BlockSpec(memory_space=pltpu.HBM)],
        out_specs=(vmem, vmem),
        scratch_shapes=[
            pltpu.VMEM(volumes.shape, volumes.dtype),
            pltpu.VMEM((2,) + listed.shape, listed.dtype),
            pltpu.SMEM((2,) + listed.shape, listed.dtype),
            pltpu.VMEM((2,) + volumes.shape[1:], volumes.dtype),
            pltpu.SemaphoreType.DMA((2,)),
            pltpu.SemaphoreType.DMA((2,)),
            pltpu.SemaphoreType.DMA((2,)),
            pltpu.SemaphoreType.DMA((2, PIECES)),
            pltpu.SemaphoreType.DMA((2, PIECES)),
        ],
        compiler_params=pltpu.CompilerParams(
            collective_id=1, has_side_effects=True, vmem_limit_bytes=57 * 2**20
        ),
        name="exchange",
    )(listed, volumes)


def pair_kernel(
    slab_count,
    pair_total,
    fields_ref,
    counts_ref,
    volumes_ref,
    above_ref,
    below_ref,
    table_x_ref,
    table_y_ref,
    win_z_ref,
    win_y_ref,
    win_x_ref,
    corr_ref,
    shift_ref,
    sums_ref,
    a_buf,
    b_buf,
    sems,
    table_buf,
    y_buf,
    c_buf,
    m_buf,
    g_buf,
):
    edge = volumes_ref.shape[1]
    lanes_all = 2 * edge
    half = edge // 2
    cap = fields_ref.shape[1]
    pitch = edge + GAP
    count = counts_ref[0]
    own_index = lax.axis_index("slab")

    def fetch(slot, start):
        buf = lax.rem(slot, 2)
        copy_a = pltpu.make_async_copy(
            volumes_ref.at[fields_ref[0, slot]], a_buf.at[buf], sems.at[0, buf]
        )
        copy_b = pltpu.make_async_copy(
            volumes_ref.at[fields_ref[2, slot]], b_buf.at[buf], sems.at[1, buf]
        )
        if not start:
            copy_a.wait()
            copy_b.wait()
            return
        copy_a.start()
        direction = fields_ref[3, slot]

        @pl.when(direction == 0)
        def _():
            copy_b.start()

        @pl.when(direction == 1)
        def _():
            pltpu.make_async_copy(above_ref, b_buf.at[buf], sems.at[1, buf]).start()

        @pl.when(direction == -1)
        def _():
            pltpu.make_async_copy(below_ref, b_buf.at[buf], sems.at[1, buf]).start()

    fetch(jnp.int32(0), True)
    corr_ref[...] = jnp.zeros_like(corr_ref)
    shift_ref[...] = jnp.zeros_like(shift_ref)
    sums_ref[...] = jnp.zeros_like(sums_ref)
    c_buf[half + 1] = jnp.zeros((edge, lanes_all), jnp.float32)
    m_buf[half + 1] = jnp.zeros((edge, lanes_all), jnp.float32)

    def pair_step(slot, _):
        buf = lax.rem(slot, 2)

        @pl.when(slot + 1 < count)
        def _():
            fetch(slot + 1, True)

        direction = fields_ref[3, slot]
        rank = jnp.int32(0)
        for other in range(cap):
            rank = rank + ((fields_ref[3, other] == direction) & (other < slot)).astype(jnp.int32)
        start_a = fields_ref[1, slot]
        start_b = jnp.where(direction == 0, fields_ref[4, slot], edge * rank)
        rows = lax.broadcasted_iota(jnp.int32, (lanes_all, 2 * lanes_all), 0)
        for part, start in enumerate((start_a, start_b)):
            where = pl.ds(part * lanes_all, lanes_all)
            inside = (rows >= start) & (rows < start + edge)
            table_buf[where, :] = jnp.where(inside, table_x_ref[where, :], 0.0).astype(jnp.bfloat16)
        fetch(slot, False)

        lanes = lax.broadcasted_iota(jnp.int32, (edge, lanes_all), 1)
        low = lanes < edge
        sign = jnp.where(low, 1.0, -1.0)

        def xy_step(step, _):
            z = CHUNK * step
            left = a_buf[buf, pl.ds(z, CHUNK)].reshape(CHUNK * edge, lanes_all)
            right = b_buf[buf, pl.ds(z, CHUNK)].reshape(CHUNK * edge, lanes_all)
            mixed = jnp.dot(
                jnp.concatenate([left, right], axis=1),
                table_buf[...],
                preferred_element_type=jnp.float32,
            )
            high, rest = split(mixed[:, :lanes_all] + mixed[:, lanes_all:])
            high = jnp.concatenate([high[k * edge : (k + 1) * edge] for k in range(CHUNK)], axis=1)
            rest = jnp.concatenate([rest[k * edge : (k + 1) * edge] for k in range(CHUNK)], axis=1)
            mixed = jnp.dot(
                table_y_ref[...],
                jnp.concatenate([high, high, rest], axis=0),
                preferred_element_type=jnp.float32,
            )
            for part in range(CHUNK):
                where = slice(part * lanes_all, (part + 1) * lanes_all)
                turned = pltpu.roll(mixed[edge:, where], edge, 1)
                y_buf[pl.ds(z + part, edge, stride=pitch), :] = mixed[:edge, where] + sign * turned
            return 0

        lax.fori_loop(0, edge // CHUNK, xy_step, 0, unroll=True)

        reversed_ids = jnp.where(low, (edge - lanes) % edge, edge + (lanes_all - lanes) % edge)

        def z_step(ky, total):
            mirror = lax.rem(edge - ky, edge)
            plane = y_buf[pl.ds(pl.multiple_of(ky * pitch, 8), edge), :]
            other = y_buf[pl.ds(pl.multiple_of(mirror * pitch, 8), edge), :]
            high, rest = split(jnp.concatenate([plane, other], axis=1))
            mixed = jnp.dot(
                table_y_ref[...],
                jnp.concatenate([high, high, rest], axis=0),
                preferred_element_type=jnp.float32,
            )
            front = mixed[:edge, :lanes_all] + sign * pltpu.roll(mixed[edge:, :lanes_all], edge, 1)
            back = mixed[:edge, lanes_all:] - sign * pltpu.roll(mixed[edge:, lanes_all:], edge, 1)
            back = jnp.take_along_axis(back, reversed_ids, axis=1)
            first = front * pltpu.roll(back, edge, 1)
            second = 0.5 * (front * front - back * back)
            cross = jnp.where(low, first, second) + pltpu.roll(
                jnp.where(low, second, first), edge, 1
            )
            square = cross * cross
            magnitude = jnp.sqrt(square + pltpu.roll(square, edge, 1))
            c_buf[ky] = cross
            m_buf[ky] = magnitude
            times = jnp.where((ky == 0) | (ky == half), 0.5, 1.0)
            return total + times * magnitude

        total = lax.fori_loop(
            0, half + 1, z_step, jnp.zeros((edge, lanes_all), jnp.float32), unroll=True
        )
        floor = jnp.sum(total) / float(edge**3) + 2.0 * EPSILON

        table_z = win_z_ref[slot]
        sign_w = sign[:WIN]

        def win_step(step, _):
            ratios = []
            for part in range(2):
                ky = 2 * step + part
                times = jnp.where((ky == 0) | (ky == half), 1.0, 2.0)
                ratios.append(times * c_buf[ky] / (m_buf[ky] + floor))
            high, rest = split(jnp.concatenate(ratios, axis=1))
            mixed = jnp.dot(
                table_z,
                jnp.concatenate([high, high, rest], axis=0),
                preferred_element_type=jnp.float32,
            )
            for part in range(2):
                where = slice(part * lanes_all, (part + 1) * lanes_all)
                g_buf[pl.ds(pl.multiple_of((2 * step + part) * WIN, 8), WIN), :] = mixed[
                    :WIN, where
                ] - sign_w * pltpu.roll(mixed[WIN:, where], edge, 1)
            return 0

        lax.fori_loop(0, half // 2 + 1, win_step, 0, unroll=True)

        planes = g_buf.shape[0] // WIN
        partial = jnp.concatenate(
            [g_buf[pl.ds(i, planes, stride=WIN), :] for i in range(WIN)], axis=1
        )
        mixed = jnp.dot(
            win_y_ref[slot][:, :planes],
            partial,
            precision=PRECISE,
            preferred_element_type=jnp.float32,
        )
        blocks = []
        for i in range(WIN):
            where = slice(i * lanes_all, (i + 1) * lanes_all)
            blocks.append(mixed[:WIN, where] - sign_w * pltpu.roll(mixed[WIN:, where], edge, 1))
        values = jnp.dot(
            jnp.concatenate(blocks, axis=0),
            win_x_ref[slot],
            precision=PRECISE,
            preferred_element_type=jnp.float32,
        )
        corr_ref[slot] = values

        weight = values * values
        line = lax.broadcasted_iota(jnp.int32, (WIN * WIN, lanes_all), 0)
        lane = lax.broadcasted_iota(jnp.int32, (WIN * WIN, lanes_all), 1)
        cells = float(WIN**3)
        energy = jnp.sum(weight, keepdims=True) / cells
        places = (line // WIN, line % WIN, lane)
        shifts = [
            (jnp.sum(weight * place.astype(jnp.float32), keepdims=True) / cells
             + energy * fields_ref[5 + axis, slot].astype(jnp.float32))
            / (energy + EPSILON)
            for axis, place in enumerate(places)
        ]
        views = sums_ref.shape[0]
        view = lax.broadcasted_iota(jnp.int32, (views, lanes_all), 0)
        entry = lax.broadcasted_iota(jnp.int32, (views, lanes_all), 1)
        center_z = (own_index.astype(jnp.float32) * edge + 0.5 * edge) / (edge * slab_count)
        center_x = (start_a.astype(jnp.float32) + 0.5 * edge) / (2.0 * edge)

        def center(index):
            return jnp.where(
                index == 0,
                center_z,
                jnp.where(index == 1, 0.5, jnp.where(index == 2, center_x, 1.0)),
            )

        hit_a = (view == fields_ref[0, slot]).astype(jnp.float32)
        hit_b = (view == fields_ref[2, slot]).astype(jnp.float32)
        normal = (hit_a + hit_b) * center(entry // 4) * center(entry % 4)
        after = jnp.maximum(entry - 16, 0)
        which = after % 3
        shift = jnp.where(which == 0, shifts[0], jnp.where(which == 1, shifts[1], shifts[2]))
        rhs = (hit_a - hit_b) * center(after // 3) * shift
        sums_ref[...] += jnp.where(entry < 16, normal, jnp.where(entry < 28, rhs, 0.0)) * (
            energy / pair_total
        )
        spot = lax.broadcasted_iota(jnp.int32, shift_ref.shape, 0)
        column = lax.broadcasted_iota(jnp.int32, shift_ref.shape, 1)
        for axis in range(3):
            shift_ref[...] += jnp.where((spot == axis) & (column == slot), shifts[axis], 0.0)
        return 0

    lax.fori_loop(0, count, pair_step, 0)


def pairs(volumes, from_above, from_below, pair_fields, pair_counts, tables, slab_count):
    view_count, edge = volumes.shape[0], volumes.shape[1]
    cap = pair_fields.shape[1]
    lanes = 2 * edge
    half = edge // 2
    table_x, table_y = static_tables(edge)
    smem = pl.BlockSpec(memory_space=pltpu.SMEM)
    vmem = pl.BlockSpec(memory_space=pltpu.VMEM)
    anywhere = pl.BlockSpec(memory_space=pltpu.HBM)

    def kernel(*refs):
        pair_kernel(slab_count, float(cap * slab_count), *refs)

    return pl.pallas_call(
        kernel,
        out_shape=(
            jax.ShapeDtypeStruct((cap, WIN * WIN, lanes), jnp.float32),
            jax.ShapeDtypeStruct((8, lanes), jnp.float32),
            jax.ShapeDtypeStruct((view_count, lanes), jnp.float32),
        ),
        in_specs=[smem, smem, anywhere, anywhere, anywhere] + [vmem] * 5,
        out_specs=(vmem, vmem, vmem),
        scratch_shapes=[
            pltpu.VMEM((2, edge, edge, lanes), volumes.dtype),
            pltpu.VMEM((2, edge, edge, lanes), volumes.dtype),
            pltpu.SemaphoreType.DMA((2, 2)),
            pltpu.VMEM((2 * lanes, 2 * lanes), jnp.bfloat16),
            pltpu.VMEM((edge * (edge + GAP), lanes), jnp.float32),
            pltpu.VMEM((half + 2, edge, lanes), jnp.float32),
            pltpu.VMEM((half + 2, edge, lanes), jnp.float32),
            pltpu.VMEM(((half + 2) * WIN, lanes), jnp.float32),
        ],
        compiler_params=pltpu.CompilerParams(vmem_limit_bytes=57 * 2**20),
        name="pairs",
    )(
        pair_fields,
        pair_counts,
        volumes,
        from_above,
        from_below,
        jnp.asarray(table_x),
        jnp.asarray(table_y),
        *tables,
    )


def sum_kernel(part_ref, out_ref, held, send_sems, recv_sems):
    count = lax.axis_size("slab")
    own = lax.axis_index("slab")
    barrier = pltpu.get_barrier_semaphore()
    for step in range(1, count):
        peer = lax.rem(own + step, count)
        pl.semaphore_signal(
            barrier, inc=1, device_id={"slab": peer}, device_id_type=pl.DeviceIdType.MESH
        )
    pl.semaphore_wait(barrier, count - 1)

    def copy_to(peer, source):
        return pltpu.make_async_remote_copy(
            src_ref=part_ref,
            dst_ref=held.at[source],
            send_sem=send_sems.at[peer],
            recv_sem=recv_sems.at[source],
            device_id={"slab": peer},
            device_id_type=pl.DeviceIdType.MESH,
        )

    for step in range(1, count):
        copy_to(lax.rem(own + step, count), own).start()
    held[own] = part_ref[...]
    for step in range(1, count):
        peer = lax.rem(own + step, count)
        copy_to(peer, own).wait_send()
        copy_to(peer, peer).wait_recv()
    total = held[0]
    for index in range(1, count):
        total = total + held[index]
    out_ref[...] = total


def summed(part):
    count = lax.axis_size("slab")
    return pl.pallas_call(
        sum_kernel,
        out_shape=jax.ShapeDtypeStruct(part.shape, part.dtype),
        in_specs=[pl.BlockSpec(memory_space=pltpu.VMEM)],
        out_specs=pl.BlockSpec(memory_space=pltpu.VMEM),
        scratch_shapes=[
            pltpu.VMEM((count,) + part.shape, part.dtype),
            pltpu.SemaphoreType.DMA((count,)),
            pltpu.SemaphoreType.DMA((count,)),
        ],
        compiler_params=pltpu.CompilerParams(collective_id=0, has_side_effects=True),
        name="slab_sum",
    )(part)


def on_device(volumes, pair_fields, pair_counts):
    cap = pair_fields.shape[1]
    edge = volumes.shape[1]
    slab_count = lax.axis_size("slab")
    live = jnp.arange(cap, dtype=jnp.int32) < pair_counts[0]
    listed = jnp.where(live[None, :], pair_fields, 0)
    listed = jnp.pad(listed, ((0, 0), (0, 2 * edge - cap)))
    tables = window_tables(pair_fields, edge)
    from_above, from_below = exchanged(volumes, listed, cap)
    corr, shifts, sums = pairs(
        volumes, from_above, from_below, pair_fields, pair_counts, tables, slab_count
    )
    sums = summed(sums)
    return (
        corr[:, :, :WIN].reshape(cap, WIN**3),
        shifts[:3, :cap],
        sums[:, :16].reshape(-1, 4, 4),
        sums[:, 16:28].reshape(-1, 4, 3),
    )


def solution(mesh):
    in_specs = (P("tm", "slab", None, None), P(None, ("tm", "slab")), P(("tm", "slab")))
    out_specs = (
        P(("tm", "slab"), None),
        P(None, ("tm", "slab")),
        P("tm", None, None),
        P("tm", None, None),
    )
    return jax.shard_map(
        on_device, mesh=mesh, in_specs=in_specs, out_specs=out_specs, check_vma=False
    )
```
